32 devices in a mesh: tok: 8 (over z, x), wid: 4 (over y, core).
Axes of the slice: x: 2, y: 2, z: 4, core: 2. Of those that a mesh axis runs over, the one named last changes fastest.
Arguments:
- acts: bfloat16 [3072, 53248], P('tok', 'wid'), may hold values from -100 to 100
- out_grads: bfloat16 [3072, 16384], P('tok', 'wid'), may hold values from -6 to 6
- test_matrix: bfloat16 [16384, 256], P('wid'), may hold values from -1 to 1
Outputs:
- coeffs: float32 [256, 16384], P('tok', 'wid')
The draws below stay inside these ranges and needn't reach their ends.
All inputs are finite; a program needn't handle non-finite values.
Results may differ from the reference program's by a relative error of at most 0.01.
Values may be sent and summed in bfloat16 or wider, within the bound.
A program may use at most 64 MiB of HBM per device.

```python
import math
import jax
import jax.numpy as jnp
from jax import lax

D = 16384
F = 53248
R = 256
TOK_DEV = 384
TOKENS = 3072
N_TOK = 8


def base_values(key, shape):
    return jnp.clip(jax.random.normal(key, shape, jnp.float32), -6.0, 6.0)


def draw_acts(key, part):
    first = jax.random.fold_in(key, 11)
    second = jax.random.fold_in(key, 12)
    values = base_values(first, (TOKENS, F))
    position = jnp.arange(F, dtype=jnp.float32) / (F - 1)
    rough = jax.random.uniform(second, (F,), jnp.float32, 0.6, 1.4)
    column = jnp.exp(position * math.log(10.0)) * rough
    scaled = values * column[None, :]
    return scaled.astype(jnp.bfloat16)


def draw_out_grads(key, part):
    first = jax.random.fold_in(key, 21)
    values = base_values(first, (TOKENS, D))
    return values.astype(jnp.bfloat16)


def draw_test_matrix(key, part):
    first = jax.random.fold_in(key, 31)
    values = base_values(first, (D, R))
    return (values * (1.0 / math.sqrt(D))).astype(jnp.bfloat16)


def setup_inputs(seed: int = 0) -> dict:
    seeds = jax.random.split(jax.random.key(seed), 4)
    acts = draw_acts(jax.random.fold_in(seeds[3], 71), 0)
    out_grads = draw_out_grads(jax.random.fold_in(seeds[3], 71), 0)
    test_matrix = draw_test_matrix(jax.random.fold_in(seeds[3], 71), 0)
    return dict(acts=acts, out_grads=out_grads, test_matrix=test_matrix)


def reference(acts, out_grads, test_matrix):
    probe = jnp.dot(out_grads.astype(jnp.float32), test_matrix.astype(jnp.float32), preferred_element_type=jnp.float32).astype(jnp.bfloat16)
    acts_blocks = acts.reshape(N_TOK, TOK_DEV, F)
    probe_blocks = probe.reshape(N_TOK, TOK_DEV, R)

    def add_block(total, pair):
        block_acts, block_probe = pair
        term = lax.dot_general(block_acts.astype(jnp.float32), block_probe.astype(jnp.float32), (((0,), (0,)), ((), ())), preferred_element_type=jnp.float32)
        term = lax.optimization_barrier(term.astype(jnp.bfloat16))
        return (total + term.astype(jnp.float32), None)
    sketch, unused = lax.scan(add_block, jnp.zeros((F, R), jnp.float32), (acts_blocks, probe_blocks))
    gram = jnp.dot(sketch.T, sketch, precision=lax.Precision.HIGHEST)
    lower = jnp.linalg.cholesky(gram)
    inverse = lax.linalg.triangular_solve(lower, jnp.eye(R, dtype=jnp.float32), left_side=True, lower=True)
    basis = jnp.dot(sketch, inverse.T, precision=lax.Precision.HIGHEST).astype(jnp.bfloat16)
    proj = jnp.dot(acts.astype(jnp.float32), basis.astype(jnp.float32), preferred_element_type=jnp.float32).astype(jnp.bfloat16)
    coeffs = lax.dot_general(proj.astype(jnp.float32), out_grads.astype(jnp.float32), (((0,), (0,)), ((), ())), preferred_element_type=jnp.float32)
    return coeffs * (1.0 / math.sqrt(TOKENS))
```

```python
import functools
import math
import types

import jax
import jax.numpy as jnp
from jax import lax
from jax.experimental import pallas as pl
from jax.experimental.pallas import tpu as pltpu
from jax.sharding import PartitionSpec as P

MESH = pl.DeviceIdType.MESH
F32 = jnp.float32
BF16 = jnp.bfloat16
HIGH = lax.Precision.HIGHEST
VMEM_LIMIT = 60 * 1024 * 1024
LINE = 4
ENDS = 2
PARTS = 2
PIECES = 16
PANELS = 8
GROUPS = 3
SKEW = 3
HOPS = GROUPS * PIECES
LAST = LINE - 1
FILL = SKEW * LAST
REDUCED = HOPS + FILL
SLOTS = HOPS + REDUCED
WAYS = (0, 1)
RING_PIECES = 4


def nt(a, b, precision=None):
    return lax.dot_general(
        a, b, (((1,), (1,)), ((), ())), preferred_element_type=F32, precision=precision
    )


def tn(a, b, precision=None):
    return lax.dot_general(
        a, b, (((0,), (0,)), ((), ())), preferred_element_type=F32, precision=precision
    )


def both(a, b):
    return jnp.logical_and(a, b)


def within(value, first, count):
    return both(value >= first, value < first + count)


class Place:
    def __init__(self, n, m):
        self.n, self.m, self.cols = n, m, n // LINE
        self.tok, self.wid = lax.axis_index("tok"), lax.axis_index("wid")
        self.z, self.x = lax.div(self.tok, self.cols), lax.rem(self.tok, self.cols)
        self.across = self.z * self.cols + 1 - self.x
        self.end = lax.div(self.z, LAST)
        self.is_end = lax.rem(self.z, LAST) == 0

    def along(self, step):
        return lax.rem(self.z + step + LINE, LINE) * self.cols + self.x

    def to_end(self, end):
        return self.z if end else LAST - self.z

    def peer(self, k):
        return lax.rem(self.wid + k, self.m)

    def barrier(self):
        sem = pltpu.get_barrier_semaphore()
        others = [{"wid": self.peer(k)} for k in range(1, self.m)]
        others += [{"tok": self.along(step)} for step in range(1, LINE)]
        others += [{"tok": self.across}]
        for other in others:
            pl.semaphore_signal(sem, inc=1, device_id=other, device_id_type=MESH)
        pl.semaphore_wait(sem, len(others))


def remote(src, dst, sems, index, device):
    return pltpu.make_async_remote_copy(
        src_ref=src,
        dst_ref=dst,
        send_sem=sems[0].at[index],
        recv_sem=sems[1].at[index],
        device_id=device,
        device_id_type=MESH,
    )


def unit_of(end, x, part):
    return (end * 2 + x) * PARTS + part


def shares(place, rows):
    share = rows // place.m
    return lambda index: pl.ds(pl.multiple_of(index * share, 16), share)


def wid_sum(place, part, got, mine, out, sems, finish):
    lines = shares(place, part.shape[0])
    me = place.wid

    def copy(phase, k):
        other = place.peer(k)
        return remote(
            mine if phase else part.at[lines(other)],
            out.at[lines(me)] if phase else got.at[k - 1],
            sems,
            (phase, k - 1),
            {"wid": other},
        )

    for k in range(1, place.m):
        copy(0, k).start()
    total = part[lines(me), :]
    for k in range(1, place.m):
        copy(0, k).wait_recv()
        total = total + got[k - 1]
    total = finish(total).astype(mine.dtype)
    mine[...] = total
    for k in range(1, place.m):
        copy(1, k).start()
    out[lines(me), :] = total
    for k in range(1, place.m):
        copy(0, k).wait_send()
        copy(1, k).wait()


def reduce_sketch(place, acts, probe, terms, line, cross, last, full, line_sems, cross_sems, last_sems):
    x, end = place.x, place.end
    width = terms.shape[-1]

    def compute(unit):
        columns = pl.ds(pl.multiple_of(unit * width, 128), width)
        term = jnp.dot(probe[...], acts[:, columns], preferred_element_type=F32)
        terms[unit] = term.astype(BF16).reshape(terms.shape[1:])

    def order(i):
        first = lax.div(i, 4)
        side = jnp.where(first == 0, 1 - x, x)
        k = lax.rem(i, 4)
        return unit_of(lax.rem(k, 2), side, 1 - lax.div(k, 2))

    def spot(end_, k):
        group, piece = lax.div(k, PIECES), lax.rem(k, PIECES)
        side = jnp.where(group == 0, 1 - x, x)
        part = jnp.where(group == GROUPS - 1, 0, 1)
        return group, piece, unit_of(end_, side, part)

    def line_copy(way, k, src):
        step = 1 if way else -1
        return remote(src, line.at[way, k], line_sems, (way, k), {"tok": place.along(step)})

    def cross_copy(way, piece):
        unit = unit_of(way, 1 - x, 0)
        return remote(
            terms.at[unit, piece], cross.at[way, piece], cross_sems, (way, piece),
            {"tok": place.across},
        )

    def last_copy(piece):
        return remote(
            line.at[end, piece], last.at[piece], last_sems, piece, {"tok": place.across}
        )

    def hop(way, k):
        pos = place.to_end(way)
        group, piece, unit = spot(way, k)

        @pl.when(pos == 0)
        def _():
            line_copy(way, k, terms.at[unit, piece]).start()

        @pl.when(pos > 0)
        def _():
            line_copy(way, k, line.at[way, k]).wait_recv()

        @pl.when(both(pos > 0, group != 1))
        def _():
            total = line[way, k].astype(F32) + terms[unit, piece].astype(F32)
            line[way, k] = total.astype(BF16)

        @pl.when(both(both(pos > 0, pos < LAST), group == 1))
        def _():
            total = line[way, k].astype(F32) + terms[unit, piece].astype(F32)
            line[way, k] = total.astype(BF16)

        @pl.when(both(pos > 0, pos < LAST))
        def _():
            line_copy(way, k, line.at[way, k]).start()

        @pl.when(both(pos == LAST, group == GROUPS - 1))
        def _():
            full[unit, piece] = line[way, k]

    lax.fori_loop(0, 3, lambda i, c: (compute(order(i)), c)[1], 0)

    def slot(s):
        @pl.when(s < 2 * PIECES)
        def _():
            cross_copy(lax.div(s, PIECES), lax.rem(s, PIECES)).start()

        for way in WAYS:
            k = s - SKEW * place.to_end(way)
            pl.when(within(k, 0, HOPS))(functools.partial(hop, way, k))

        pl.when(within(s, 0, 5))(lambda: compute(order(s + 3)))

        @pl.when(within(s, 2 * PIECES - 2, PIECES))
        def _():
            piece = s - (2 * PIECES - 2)
            for way in WAYS:
                cross_copy(way, piece).wait_recv()
                unit = unit_of(way, x, 0)
                total = terms[unit, piece].astype(F32) + cross[way, piece].astype(F32)
                terms[unit, piece] = total.astype(BF16)

        @pl.when(both(place.is_end, within(s, 2 * PIECES - 3, PIECES)))
        def _():
            last_copy(s - (2 * PIECES - 3)).start()

        @pl.when(both(place.is_end, within(s, REDUCED - PIECES, PIECES)))
        def _():
            piece = s - (REDUCED - PIECES)
            last_copy(piece).wait_recv()
            unit = unit_of(end, x, 1)
            total = line[end, PIECES + piece].astype(F32) + last[piece].astype(F32)
            total = total + terms[unit, piece].astype(F32)
            full[unit, piece] = total.astype(BF16)

    def drain():
        for way in WAYS:
            sent = place.to_end(way) < LAST

            @pl.when(sent)
            def _():
                def one(k, carry):
                    line_copy(way, k, line.at[way, k]).wait_send()
                    return carry

                lax.fori_loop(0, HOPS, one, 0)

        def one(k, carry):
            for way in WAYS:
                cross_copy(way, k).wait_send()
            pl.when(place.is_end)(lambda: last_copy(k).wait_send())
            return carry

        lax.fori_loop(0, PIECES, one, 0)

    return slot, drain


class Gram:
    def __init__(self, place, part, got, share, crossed, ends, mine, gram, sems):
        self.place, self.part, self.got, self.share = place, part, got, share
        self.crossed, self.ends, self.mine, self.gram = crossed, ends, mine, gram
        self.wid_sems, self.cross_sems, self.end_sems = sems
        self.lines = shares(place, gram.shape[0])

    def first(self, k):
        other = self.place.peer(k)
        return remote(
            self.part.at[self.lines(other)], self.got.at[k - 1], self.wid_sems, (0, k - 1),
            {"wid": other},
        )

    def over_x(self):
        return remote(
            self.share, self.crossed, self.cross_sems, 0, {"tok": self.place.across}
        )

    def over_z(self, step, end):
        send, recv = self.end_sems
        return pltpu.make_async_remote_copy(
            src_ref=self.ends.at[end],
            dst_ref=self.ends.at[end],
            send_sem=send.at[step - 1],
            recv_sem=recv.at[end],
            device_id={"tok": self.place.along(step)},
            device_id_type=MESH,
        )

    def spread(self, k):
        return remote(
            self.mine, self.gram.at[self.lines(self.place.wid)], self.wid_sems, (1, k - 1),
            {"wid": self.place.peer(k)},
        )

    def start(self, full):
        @pl.when(self.place.is_end)
        def _():
            rank, width = self.part.shape[0], full.shape[-1]
            unit = unit_of(self.place.end, self.place.x, 0)
            a = full[unit].reshape(rank, width)
            b = full[unit + 1].reshape(rank, width)
            self.part[...] = nt(a, a) + nt(b, b)
            for k in range(1, self.place.m):
                self.first(k).start()

    def cross(self):
        @pl.when(self.place.is_end)
        def _():
            total = self.part[self.lines(self.place.wid), :]
            for k in range(1, self.place.m):
                self.first(k).wait_recv()
                total = total + self.got[k - 1]
            self.share[...] = total
            self.over_x().start()

    def along(self):
        @pl.when(self.place.is_end)
        def _():
            self.over_x().wait_recv()
            self.ends[self.place.end] = self.share[...] + self.crossed[...]
            for step in range(1, LINE):
                self.over_z(step, self.place.end).start()

    def gather(self):
        for end in range(ENDS):
            @pl.when(self.place.z != end * LAST)
            def _():
                self.over_z(1, end).wait_recv()

        total = self.ends[0] + self.ends[1]
        self.mine[...] = total
        for k in range(1, self.place.m):
            self.spread(k).start()
        self.gram[self.lines(self.place.wid), :] = total

    def finish(self):
        for k in range(1, self.place.m):
            self.spread(k).wait_recv()

    def drain(self):
        @pl.when(self.place.is_end)
        def _():
            for k in range(1, self.place.m):
                self.first(k).wait_send()
            self.over_x().wait_send()
            for step in range(1, LINE):
                self.over_z(step, self.place.end).wait_send()

        for k in range(1, self.place.m):
            self.spread(k).wait_send()


def gather_sketch(place, acts, full, mixed, gram, rest, lower, inverse, line_sems, forward_sems, swap_sems):
    x, end = place.x, place.end
    rank, width = rest.shape[0], full.shape[-1]
    panel = rank // PANELS
    levels = (rank - 1).bit_length()
    solve_at = FILL + 17
    invert_at = solve_at + 2 * PANELS

    def spot(end_, k):
        group, piece = lax.div(k, PIECES), lax.rem(k, PIECES)
        side = jnp.where(group == GROUPS - 1, 1 - x, x)
        part = jnp.where(group == 0, 0, 1)
        return group, piece, unit_of(end_, side, part)

    def copy(unit, piece, sems, index, device):
        block = full.at[unit, piece]
        return remote(block, block, sems, index, {"tok": device})

    def line_copy(way, k):
        group, piece, unit = spot(way, k)
        return copy(unit, piece, line_sems, (way, k), place.along(-1 if way else 1))

    def forward_copy(way, piece):
        return copy(unit_of(way, x, 0), piece, forward_sems, (way, piece), place.across)

    def swap_copy(piece):
        return copy(unit_of(end, x, 1), piece, swap_sems, piece, place.across)

    def hop(way, k):
        pos = place.to_end(1 - way)
        group, piece, unit = spot(way, k)

        @pl.when(pos > 0)
        def _():
            line_copy(way, k).wait_recv()

        @pl.when(both(pos == 0, group == GROUPS - 1))
        def _():
            swap_copy(piece).wait_recv()

        @pl.when(pos < LAST)
        def _():
            line_copy(way, k).start()

    def add(unit):
        columns = pl.ds(pl.multiple_of(unit * width, 128), width)
        mixed[...] += nt(acts[:, columns], full[unit].reshape(rank, width))

    mixed[...] = jnp.zeros_like(mixed)

    def slot(s):
        @pl.when(both(place.is_end, within(s, 0, PIECES)))
        def _():
            swap_copy(s).start()

        for way in WAYS:
            k = s - SKEW * place.to_end(1 - way)
            pl.when(within(k, 0, HOPS))(functools.partial(hop, way, k))
            sent = s - FILL - way * PIECES
            pl.when(within(sent, 0, PIECES))(lambda: forward_copy(way, sent).start())
            came = sent - 4
            pl.when(within(came, 0, PIECES))(lambda: forward_copy(way, came).wait_recv())

        pl.when(s == FILL)(lambda: gram.start(full))
        pl.when(s == FILL + 4)(gram.cross)
        pl.when(s == FILL + 7)(gram.along)
        pl.when(s == FILL + 12)(gram.gather)

        @pl.when(s == solve_at - 1)
        def _():
            gram.finish()
            rest[...] = gram.gram[...]

        solve = s - solve_at
        for half in range(2):
            pl.when(both(within(solve, 0, 2 * PANELS), lax.rem(solve, 2) == half))(
                lambda: factor_panel(lax.div(solve, 2), half, panel, rest, inverse)
            )

        @pl.when(s == invert_at)
        def _():
            lower[...] = inverse[...].T
            start_invert(lower, inverse)

        pl.when(within(s, invert_at, levels))(
            lambda: invert_level(s - invert_at, lower, inverse)
        )
        for way in WAYS:
            pl.when(s == PIECES + FILL + way)(lambda: add(unit_of(way, x, 0)))
            pl.when(s == 2 * PIECES + FILL + way)(lambda: add(unit_of(way, x, 1)))
            pl.when(s == (way + 1) * PIECES + FILL + 4)(lambda: add(unit_of(way, 1 - x, 0)))

    def finish():
        for way in WAYS:
            add(unit_of(way, 1 - x, 1))

    def drain():
        for way in WAYS:
            @pl.when(place.to_end(1 - way) < LAST)
            def _():
                def one(k, carry):
                    line_copy(way, k).wait_send()
                    return carry

                lax.fori_loop(0, HOPS, one, 0)

        def one(k, carry):
            for way in WAYS:
                forward_copy(way, k).wait_send()
            pl.when(place.is_end)(lambda: swap_copy(k).wait_send())
            return carry

        lax.fori_loop(0, PIECES, one, 0)

    return slot, finish, drain


def factor_panel(k, half, block, rest, upper):
    size = rest.shape[0]
    lane = lax.broadcasted_iota(jnp.int32, (block, size), 1)
    line = lax.broadcasted_iota(jnp.int32, (block, size), 0)
    one_line = lax.broadcasted_iota(jnp.int32, (block, 1), 0)
    first = pl.multiple_of(k * block, block)
    rows = rest[pl.ds(first, block), :]
    for j in range(half * block // 2, (half + 1) * block // 2):
        picked = jnp.where(lane == first + j, rows, 0.0)
        column = jnp.sum(picked, axis=1, keepdims=True)
        ratio = jnp.where(one_line > j, column / column[j : j + 1, :], 0.0)
        rows = rows - ratio * rows[j : j + 1, :]
    if half == 0:
        rest[pl.ds(first, block), :] = rows
        return
    diagonal = jnp.sum(
        jnp.where(lane == first + line, rows, 0.0), axis=1, keepdims=True
    )
    rows = jnp.where(lane >= first + line, rows / jnp.sqrt(diagonal), 0.0)
    upper[pl.ds(first, block), :] = rows
    rest[...] -= tn(rows, rows, HIGH)


def start_invert(lower, inverse):
    i = lax.broadcasted_iota(jnp.int32, lower.shape, 0)
    j = lax.broadcasted_iota(jnp.int32, lower.shape, 1)
    inverse[...] = jnp.where(i == j, 1.0 / jnp.where(i == j, lower[...], 1.0), 0.0)


def invert_level(k, lower, inverse):
    i = lax.broadcasted_iota(jnp.int32, lower.shape, 0)
    j = lax.broadcasted_iota(jnp.int32, lower.shape, 1)
    i_block, j_block = lax.shift_right_logical(i, k), lax.shift_right_logical(j, k)
    same = lax.shift_right_logical(i, k + 1) == lax.shift_right_logical(j, k + 1)
    below = jnp.where(jnp.logical_and(same, i_block > j_block), lower[...], 0.0)
    right = jnp.dot(below, inverse[...], precision=HIGH, preferred_element_type=F32)
    inverse[...] -= jnp.dot(inverse[...], right, precision=HIGH, preferred_element_type=F32)


class Ring:
    def __init__(self, n):
        self.n, self.rows, self.cols = n, LINE, n // LINE
        self.body = self.rows * (self.cols - 1)
        self.tok = lax.axis_index("tok")
        self.pos = self.pos_of(self.tok)

    def pos_of(self, tok):
        r, c = lax.div(tok, self.cols), lax.rem(tok, self.cols)
        odd = lax.rem(r, 2)
        inner = lax.div(c + self.cols - 1, self.cols)
        along = r * (self.cols - 1) + (1 - odd) * (c - 1) + odd * (self.cols - 1 - c)
        back = self.body + self.rows - 1 - r
        return inner * along + (1 - inner) * back

    def tok_of(self, pos):
        last = lax.div(pos, self.body)
        r, k = lax.div(pos, self.cols - 1), lax.rem(pos, self.cols - 1)
        odd = lax.rem(r, 2)
        along = r * self.cols + (1 - odd) * (k + 1) + odd * (self.cols - 1 - k)
        back = (self.rows - 1 - (pos - self.body)) * self.cols
        return (1 - last) * along + last * back

    def at(self, offset):
        return lax.rem(self.pos + offset + 2 * self.n, self.n)

    def neighbours(self):
        return self.tok_of(self.at(1)), self.tok_of(self.at(-1))


def ring_scatter(ring, term, store, send, recv, sems):
    n = ring.n
    dest = ring.neighbours()

    def copy(way, step, piece):
        return remote(
            send.at[way, step, piece], recv.at[way, step, piece], sems, (way, step, piece),
            {"tok": dest[way]},
        )

    def block(way, step):
        return ring.at(-1 - step) if way == 0 else ring.at(1 + step)

    for piece in range(RING_PIECES):
        for way in WAYS:
            send[way, 0, piece] = term(way, piece, block(way, 0)).astype(BF16)
            copy(way, 0, piece).start()

    def step(s, carry):
        for piece in range(RING_PIECES):
            for way in WAYS:
                own = term(way, piece, block(way, s))
                copy(way, s - 1, piece).wait_recv()
                total = own + recv[way, s - 1, piece].astype(F32)
                send[way, s, piece] = total.astype(BF16)
                copy(way, s, piece).start()
        return carry

    lax.fori_loop(1, n - 1, step, 0)
    for piece in range(RING_PIECES):
        for way in WAYS:
            own = term(way, piece, ring.pos)
            copy(way, n - 2, piece).wait_recv()
            store(way, piece, own + recv[way, n - 2, piece].astype(F32))

    def drain(s, carry):
        for piece in range(RING_PIECES):
            for way in WAYS:
                copy(way, s, piece).wait_send()
        return carry

    lax.fori_loop(0, n - 1, drain, 0)


def coeffs(place, proj, grads, out, terms, send, recv, sems, scale):
    ring = Ring(place.n)
    rows, width = out.shape
    part = width // (2 * RING_PIECES)

    def term(way, piece, pos):
        first = (way * RING_PIECES + piece) * part
        return terms[ring.tok_of(pos), :, first : first + part]

    def store(way, piece, total):
        first = (way * RING_PIECES + piece) * part
        out[:, first : first + part] = total

    for first in range(0, width, part):
        last = first + part
        piece = tn(proj[...], grads[:, first:last])
        terms[:, :, first:last] = (piece * scale).reshape(place.n, rows, part)
    ring_scatter(ring, term, store, send, recv, sems)


def kernel(n, m, scale, names, acts_in, grads_in, test_in, out, *refs):
    s = types.SimpleNamespace(**dict(zip(names, refs)))
    place = Place(n, m)
    loads = [
        pltpu.make_async_copy(src, dst, s.load_sems.at[i])
        for i, (src, dst) in enumerate(
            ((grads_in, s.grads), (test_in, s.test), (acts_in, s.acts))
        )
    ]
    for load in loads:
        load.start()
    place.barrier()
    loads[0].wait()
    loads[1].wait()
    s.probe_part[...] = jnp.dot(s.grads[...], s.test[...], preferred_element_type=F32).T
    wid_sum(
        place, s.probe_part, s.probe_got, s.probe_mine, s.probe,
        (s.probe_send, s.probe_recv), lambda total: total,
    )
    loads[2].wait()
    reduce_slot, drain_reduce = reduce_sketch(
        place, s.acts, s.probe, s.terms, s.line, s.cross, s.last, s.full,
        (s.line_send, s.line_recv), (s.cross_send, s.cross_recv), (s.last_send, s.last_recv),
    )
    gram = Gram(
        place, s.gram_part, s.gram_got, s.gram_share, s.gram_cross, s.gram_ends,
        s.gram_mine, s.gram,
        (
            (s.gram_send, s.gram_recv), (s.gram_x_send, s.gram_x_recv),
            (s.gram_z_send, s.gram_z_recv),
        ),
    )
    gather_slot, finish_gather, drain_gather = gather_sketch(
        place, s.acts, s.full, s.mixed, gram, s.rest, s.lower, s.inverse,
        (s.back_send, s.back_recv), (s.forward_send, s.forward_recv),
        (s.swap_send, s.swap_recv),
    )

    def slot(i, carry):
        reduce_slot(i)
        gather_slot(i - HOPS)
        return carry

    lax.fori_loop(0, SLOTS, slot, 0)
    finish_gather()
    wid_sum(
        place, s.mixed, s.mixed_got, s.proj_mine, s.proj, (s.mixed_send, s.mixed_recv),
        lambda total: nt(total, s.inverse[...], HIGH),
    )
    coeffs(
        place, s.proj, s.grads, out, s.out_terms, s.ring_from, s.ring_to,
        (s.ring_send, s.ring_recv), scale,
    )
    drain_reduce()
    drain_gather()
    gram.drain()


def scratch_of(n, m, tokens, hidden, rank, model):
    units = ENDS * 2 * PARTS
    block = (rank // PIECES, hidden // units)
    vmem, dma = pltpu.VMEM, pltpu.SemaphoreType.DMA
    rows = rank // n
    part = model // (2 * RING_PIECES)

    def pair(name, shape):
        return {name + "_send": dma(shape), name + "_recv": dma(shape)}

    return {
        "acts": vmem((tokens, hidden), BF16),
        "grads": vmem((tokens, model), BF16),
        "test": vmem((model, rank), BF16),
        "load_sems": dma((3,)),
        "probe_part": vmem((rank, tokens), F32),
        "probe_got": vmem((m - 1, rank // m, tokens), F32),
        "probe_mine": vmem((rank // m, tokens), BF16),
        "probe": vmem((rank, tokens), BF16),
        **pair("probe", (2, m - 1)),
        "terms": vmem((units, PIECES, *block), BF16),
        "line": vmem((ENDS, HOPS, *block), BF16),
        "cross": vmem((ENDS, PIECES, *block), BF16),
        "last": vmem((PIECES, *block), BF16),
        "full": vmem((units, PIECES, *block), BF16),
        **pair("line", (ENDS, HOPS)),
        **pair("cross", (ENDS, PIECES)),
        **pair("last", (PIECES,)),
        "gram_part": vmem((rank, rank), F32),
        "gram_got": vmem((m - 1, rank // m, rank), F32),
        "gram_share": vmem((rank // m, rank), F32),
        "gram_cross": vmem((rank // m, rank), F32),
        "gram_ends": vmem((ENDS, rank // m, rank), F32),
        "gram_mine": vmem((rank // m, rank), F32),
        "gram": vmem((rank, rank), F32),
        **pair("gram", (2, m - 1)),
        **pair("gram_x", (1,)),
        "gram_z_send": dma((LAST,)),
        "gram_z_recv": dma((ENDS,)),
        "mixed": vmem((tokens, rank), F32),
        "rest": vmem((rank, rank), F32),
        "lower": vmem((rank, rank), F32),
        "inverse": vmem((rank, rank), F32),
        **pair("back", (ENDS, HOPS)),
        **pair("forward", (ENDS, PIECES)),
        **pair("swap", (PIECES,)),
        "mixed_got": vmem((m - 1, tokens // m, rank), F32),
        "proj_mine": vmem((tokens // m, rank), BF16),
        "proj": vmem((tokens, rank), BF16),
        **pair("mixed", (2, m - 1)),
        "out_terms": vmem((n, rows, model), F32),
        "ring_from": vmem((2, n - 1, RING_PIECES, rows, part), BF16),
        "ring_to": vmem((2, n - 1, RING_PIECES, rows, part), BF16),
        **pair("ring", (2, n - 1, RING_PIECES)),
    }


def line_shards(n, m, acts, out_grads, test_matrix):
    tokens, hidden = acts.shape
    rank, model = test_matrix.shape[1], out_grads.shape[1]
    scratch = scratch_of(n, m, tokens, hidden, rank, model)
    scale = 1.0 / math.sqrt(tokens * n)
    return pl.pallas_call(
        functools.partial(kernel, n, m, scale, tuple(scratch)),
        out_shape=jax.ShapeDtypeStruct((rank // n, model), F32),
        in_specs=[pl.BlockSpec(memory_space=pl.ANY)] * 3,
        out_specs=pl.BlockSpec(memory_space=pltpu.VMEM),
        scratch_shapes=list(scratch.values()),
        compiler_params=pltpu.CompilerParams(
            collective_id=0, has_side_effects=True, vmem_limit_bytes=VMEM_LIMIT
        ),
    )(acts, out_grads, test_matrix)


def factor_inverse(gram):
    lower = jnp.linalg.cholesky(gram)
    eye_matrix = jnp.eye(gram.shape[0], dtype=F32)
    return lax.linalg.triangular_solve(lower, eye_matrix, left_side=True, lower=True)


def plain_shards(acts, out_grads, test_matrix):
    partial_probe = jnp.dot(out_grads, test_matrix, preferred_element_type=F32)
    probe = lax.psum(partial_probe, "wid").astype(BF16)
    local_sketch = lax.dot_general(
        acts, probe, (((0,), (0,)), ((), ())), preferred_element_type=F32
    )
    sketch = lax.psum(local_sketch.astype(BF16), "tok")
    gram = lax.psum(
        lax.dot_general(sketch, sketch, (((0,), (0,)), ((), ())), preferred_element_type=F32),
        "wid",
    )
    inverse = factor_inverse(gram)
    mixed = lax.psum(jnp.dot(acts, sketch, preferred_element_type=F32), "wid")
    proj = jnp.dot(mixed, inverse.T, precision=lax.Precision.HIGHEST).astype(BF16)
    scale = 1.0 / math.sqrt(acts.shape[0] * lax.axis_size("tok"))
    term = lax.dot_general(
        proj, out_grads, (((0,), (0,)), ((), ())), preferred_element_type=F32
    )
    return lax.psum_scatter(term * scale, "tok", scatter_dimension=0, tiled=True)


def solution(mesh):
    n, m = mesh.shape["tok"], mesh.shape["wid"]

    def shards(acts, out_grads, test_matrix):
        tokens, hidden = acts.shape
        model, rank = test_matrix.shape
        fits = (
            n == 2 * LINE
            and m > 1
            and tokens % (16 * m) == 0
            and rank % (16 * m) == 0
            and rank % (16 * PIECES) == 0
            and rank % (16 * n) == 0
            and rank <= 512
            and hidden % (ENDS * 2 * PARTS * 128) == 0
            and model % (2 * RING_PIECES * 128) == 0
            and (tokens * hidden + 2 * rank * hidden) * 2 < VMEM_LIMIT // 2
        )
        if fits:
            return line_shards(n, m, acts, out_grads, test_matrix)
        return plain_shards(acts, out_grads, test_matrix)

    return jax.shard_map(
        shards,
        mesh=mesh,
        in_specs=(P("tok", "wid"), P("tok", "wid"), P("wid", None)),
        out_specs=P("tok", "wid"),
        check_vma=False,
    )
```

```python
import functools
import math
import types

import jax
import jax.numpy as jnp
from jax import lax
from jax.experimental import pallas as pl
from jax.experimental.pallas import tpu as pltpu
from jax.sharding import PartitionSpec as P

MESH = pl.DeviceIdType.MESH
F32 = jnp.float32
BF16 = jnp.bfloat16
HIGH = lax.Precision.HIGHEST
VMEM_LIMIT = 60 * 1024 * 1024
LINE = 4
ENDS = 2
PARTS = 2
PIECES = 16
PANELS = 8
TURNS = 2
STEP = 8
GROUPS = 3
SKEW = 5
HOPS = GROUPS * PIECES
LAST = LINE - 1
FILL = SKEW * LAST
REDUCED = HOPS + FILL
SLOTS = HOPS + REDUCED
WAYS = (0, 1)
RING_PIECES = 4


def nt(a, b, precision=None):
    return lax.dot_general(
        a, b, (((1,), (1,)), ((), ())), preferred_element_type=F32, precision=precision
    )


def tn(a, b, precision=None):
    return lax.dot_general(
        a, b, (((0,), (0,)), ((), ())), preferred_element_type=F32, precision=precision
    )


def both(a, b):
    return jnp.logical_and(a, b)


def within(value, first, count):
    return both(value >= first, value < first + count)


class Place:
    def __init__(self, n, m):
        self.n, self.m, self.cols = n, m, n // LINE
        self.tok, self.wid = lax.axis_index("tok"), lax.axis_index("wid")
        self.z, self.x = lax.div(self.tok, self.cols), lax.rem(self.tok, self.cols)
        self.across = self.z * self.cols + 1 - self.x
        self.end = lax.div(self.z, LAST)
        self.is_end = lax.rem(self.z, LAST) == 0

    def along(self, step):
        return lax.rem(self.z + step + LINE, LINE) * self.cols + self.x

    def to_end(self, end):
        return self.z if end else LAST - self.z

    def peer(self, k):
        return lax.rem(self.wid + k, self.m)

    def barrier(self):
        sem = pltpu.get_barrier_semaphore()
        others = [{"wid": self.peer(k)} for k in range(1, self.m)]
        others += [{"tok": self.along(step)} for step in range(1, LINE)]
        others += [{"tok": self.across}]
        for other in others:
            pl.semaphore_signal(sem, inc=1, device_id=other, device_id_type=MESH)
        pl.semaphore_wait(sem, len(others))


def remote(src, dst, sems, index, device):
    return pltpu.make_async_remote_copy(
        src_ref=src,
        dst_ref=dst,
        send_sem=sems[0].at[index],
        recv_sem=sems[1].at[index],
        device_id=device,
        device_id_type=MESH,
    )


def unit_of(end, x, part):
    return (end * 2 + x) * PARTS + part


def shares(place, rows):
    share = rows // place.m
    return lambda index: pl.ds(pl.multiple_of(index * share, 16), share)


def wid_sum(place, part, got, mine, out, sems, finish):
    lines = shares(place, part.shape[0])
    me = place.wid

    def copy(phase, k):
        other = place.peer(k)
        return remote(
            mine if phase else part.at[lines(other)],
            out.at[lines(me)] if phase else got.at[k - 1],
            sems,
            (phase, k - 1),
            {"wid": other},
        )

    for k in range(1, place.m):
        copy(0, k).start()
    total = part[lines(me), :]
    for k in range(1, place.m):
        copy(0, k).wait_recv()
        total = total + got[k - 1]
    total = finish(total).astype(mine.dtype)
    mine[...] = total
    for k in range(1, place.m):
        copy(1, k).start()
    out[lines(me), :] = total
    for k in range(1, place.m):
        copy(0, k).wait_send()
        copy(1, k).wait()


def reduce_sketch(place, acts, probe, terms, line, cross, last, full, line_sems, cross_sems, last_sems):
    x, end = place.x, place.end
    width = terms.shape[-1]

    def compute(unit):
        columns = pl.ds(pl.multiple_of(unit * width, 128), width)
        term = jnp.dot(probe[...], acts[:, columns], preferred_element_type=F32)
        terms[unit] = term.astype(BF16).reshape(terms.shape[1:])

    def order(i):
        side = jnp.where(lax.div(i, 4) == 0, 1 - x, x)
        k = lax.rem(i, 4)
        own = lax.div(k, 2)
        return unit_of(lax.rem(1 - end + own, 2), side, 1 - lax.rem(k, 2))

    def spot(end_, k):
        group, piece = lax.div(k, PIECES), lax.rem(k, PIECES)
        side = jnp.where(group == 0, 1 - x, x)
        part = jnp.where(group == GROUPS - 1, 0, 1)
        return group, piece, unit_of(end_, side, part)

    def line_copy(way, k, src):
        step = 1 if way else -1
        return remote(src, line.at[way, k], line_sems, (way, k), {"tok": place.along(step)})

    def cross_copy(way, piece):
        unit = unit_of(way, 1 - x, 0)
        return remote(
            terms.at[unit, piece], cross.at[way, piece], cross_sems, (way, piece),
            {"tok": place.across},
        )

    def last_copy(piece):
        return remote(
            line.at[end, piece], last.at[piece], last_sems, piece, {"tok": place.across}
        )

    def hop(way, k):
        pos = place.to_end(way)
        group, piece, unit = spot(way, k)

        @pl.when(pos == 0)
        def _():
            line_copy(way, k, terms.at[unit, piece]).start()

        @pl.when(pos > 0)
        def _():
            line_copy(way, k, line.at[way, k]).wait_recv()

        @pl.when(both(pos > 0, group != 1))
        def _():
            total = line[way, k].astype(F32) + terms[unit, piece].astype(F32)
            line[way, k] = total.astype(BF16)

        @pl.when(both(both(pos > 0, pos < LAST), group == 1))
        def _():
            total = line[way, k].astype(F32) + terms[unit, piece].astype(F32)
            line[way, k] = total.astype(BF16)

        @pl.when(both(pos > 0, pos < LAST))
        def _():
            line_copy(way, k, line.at[way, k]).start()

        @pl.when(both(pos == LAST, group == GROUPS - 1))
        def _():
            full[unit, piece] = line[way, k]

    compute(order(0))

    def slot(s):
        for way in WAYS:
            k = s - SKEW * place.to_end(way)
            pl.when(within(k, 0, HOPS))(functools.partial(hop, way, k))

        pl.when(within(s, 0, 7))(lambda: compute(order(s + 1)))

        @pl.when(s < 2 * PIECES)
        def _():
            first = lax.rem(1 - end + lax.div(s, PIECES), 2)
            cross_copy(first, lax.rem(s, PIECES)).start()

        @pl.when(within(s, 2 * PIECES - 2, PIECES))
        def _():
            piece = s - (2 * PIECES - 2)
            for way in WAYS:
                cross_copy(way, piece).wait_recv()
                unit = unit_of(way, x, 0)
                total = terms[unit, piece].astype(F32) + cross[way, piece].astype(F32)
                terms[unit, piece] = total.astype(BF16)

        @pl.when(both(place.is_end, within(s, 2 * PIECES - 3, PIECES)))
        def _():
            last_copy(s - (2 * PIECES - 3)).start()

        @pl.when(both(place.is_end, within(s, REDUCED - PIECES, PIECES)))
        def _():
            piece = s - (REDUCED - PIECES)
            last_copy(piece).wait_recv()
            unit = unit_of(end, x, 1)
            total = line[end, PIECES + piece].astype(F32) + last[piece].astype(F32)
            total = total + terms[unit, piece].astype(F32)
            full[unit, piece] = total.astype(BF16)

    def drain():
        for way in WAYS:
            sent = place.to_end(way) < LAST

            @pl.when(sent)
            def _():
                def one(k, carry):
                    line_copy(way, k, line.at[way, k]).wait_send()
                    return carry

                lax.fori_loop(0, HOPS, one, 0)

        def one(k, carry):
            for way in WAYS:
                cross_copy(way, k).wait_send()
            pl.when(place.is_end)(lambda: last_copy(k).wait_send())
            return carry

        lax.fori_loop(0, PIECES, one, 0)

    return slot, drain


class Gram:
    def __init__(self, place, part, got, share, crossed, ends, mine, gram, sems):
        self.place, self.part, self.got, self.share = place, part, got, share
        self.crossed, self.ends, self.mine, self.gram = crossed, ends, mine, gram
        self.wid_sems, self.cross_sems, self.end_sems = sems
        self.lines = shares(place, gram.shape[0])

    def first(self, k):
        other = self.place.peer(k)
        return remote(
            self.part.at[self.lines(other)], self.got.at[k - 1], self.wid_sems, (0, k - 1),
            {"wid": other},
        )

    def over_x(self):
        return remote(
            self.share, self.crossed, self.cross_sems, 0, {"tok": self.place.across}
        )

    def over_z(self, end):
        block = self.ends.at[end]
        step = -1 if end else 1
        return remote(block, block, self.end_sems, end, {"tok": self.place.along(step)})

    def spread(self, k):
        return remote(
            self.mine, self.gram.at[self.lines(self.place.wid)], self.wid_sems, (1, k - 1),
            {"wid": self.place.peer(k)},
        )

    def start(self, full):
        @pl.when(self.place.is_end)
        def _():
            rank, width = self.part.shape[0], full.shape[-1]
            unit = unit_of(self.place.end, self.place.x, 0)
            a = full[unit].reshape(rank, width)
            b = full[unit + 1].reshape(rank, width)
            self.part[...] = nt(a, a) + nt(b, b)
            for k in range(1, self.place.m):
                self.first(k).start()

    def cross(self):
        @pl.when(self.place.is_end)
        def _():
            total = self.part[self.lines(self.place.wid), :]
            for k in range(1, self.place.m):
                self.first(k).wait_recv()
                total = total + self.got[k - 1]
            self.share[...] = total
            self.over_x().start()

    def along(self):
        @pl.when(self.place.is_end)
        def _():
            self.over_x().wait_recv()
            self.ends[self.place.end] = self.share[...] + self.crossed[...]
            for end in range(ENDS):
                pl.when(self.place.end == end)(lambda: self.over_z(end).start())

    def relay(self, step):
        for end in range(ENDS):
            @pl.when(self.place.to_end(1 - end) == step)
            def _():
                self.over_z(end).wait_recv()
                if step < LAST:
                    self.over_z(end).start()

    def gather(self):
        self.relay(LAST)
        total = self.ends[0] + self.ends[1]
        self.mine[...] = total
        for k in range(1, self.place.m):
            self.spread(k).start()
        self.gram[self.lines(self.place.wid), :] = total

    def finish(self):
        for k in range(1, self.place.m):
            self.spread(k).wait_recv()

    def drain(self):
        @pl.when(self.place.is_end)
        def _():
            for k in range(1, self.place.m):
                self.first(k).wait_send()
            self.over_x().wait_send()

        for end in range(ENDS):
            pl.when(self.place.to_end(1 - end) < LAST)(
                lambda: self.over_z(end).wait_send()
            )
        for k in range(1, self.place.m):
            self.spread(k).wait_send()


def gather_sketch(place, acts, full, mixed, gram, rest, right, inverse, line_sems, forward_sems, swap_sems):
    x, end = place.x, place.end
    rank, width = rest.shape[0], full.shape[-1]
    solve_at = FILL + 29

    def spot(end_, k):
        group, piece = lax.div(k, PIECES), lax.rem(k, PIECES)
        side = jnp.where(group == GROUPS - 1, 1 - x, x)
        part = jnp.where(group == 0, 0, 1)
        return group, piece, unit_of(end_, side, part)

    def copy(unit, piece, sems, index, device):
        block = full.at[unit, piece]
        return remote(block, block, sems, index, {"tok": device})

    def line_copy(way, k):
        group, piece, unit = spot(way, k)
        return copy(unit, piece, line_sems, (way, k), place.along(-1 if way else 1))

    def forward_copy(way, piece):
        return copy(unit_of(way, x, 0), piece, forward_sems, (way, piece), place.across)

    def swap_copy(piece):
        return copy(unit_of(end, x, 1), piece, swap_sems, piece, place.across)

    def hop(way, k):
        pos = place.to_end(1 - way)
        group, piece, unit = spot(way, k)

        @pl.when(pos > 0)
        def _():
            line_copy(way, k).wait_recv()

        @pl.when(both(pos == 0, group == GROUPS - 1))
        def _():
            swap_copy(piece).wait_recv()

        @pl.when(pos < LAST)
        def _():
            line_copy(way, k).start()

    def add(unit):
        columns = pl.ds(pl.multiple_of(unit * width, 128), width)
        mixed[...] += nt(acts[:, columns], full[unit].reshape(rank, width))

    mixed[...] = jnp.zeros_like(mixed)

    def slot(s):
        @pl.when(both(place.is_end, within(s, 0, PIECES)))
        def _():
            swap_copy(s).start()

        for way in WAYS:
            k = s - SKEW * place.to_end(1 - way)
            pl.when(within(k, 0, HOPS))(functools.partial(hop, way, k))
            sent = s - FILL - way * PIECES
            pl.when(within(sent, 0, PIECES))(lambda: forward_copy(way, sent).start())
            came = sent - 12
            pl.when(within(came, 0, PIECES))(lambda: forward_copy(way, came).wait_recv())

        pl.when(s == FILL)(lambda: gram.start(full))
        pl.when(s == FILL + 4)(gram.cross)
        pl.when(s == FILL + 9)(gram.along)
        for step in range(1, LAST):
            pl.when(s == FILL + 9 + 5 * step)(lambda: gram.relay(step))
        pl.when(s == FILL + 9 + 5 * LAST)(gram.gather)

        @pl.when(s == solve_at - 1)
        def _():
            gram.finish()
            start_solve(gram.gram, rest, right)

        solve = s - solve_at
        for part in range(TURNS):
            mine = both(within(solve, 0, TURNS * PANELS), lax.rem(solve, TURNS) == part)
            pl.when(mine)(
                lambda: solve_part(lax.div(solve, TURNS), part, rest, right, inverse)
            )

        for way in WAYS:
            pl.when(s == PIECES + FILL + way)(lambda: add(unit_of(way, x, 0)))
            pl.when(s == 2 * PIECES + FILL + way)(lambda: add(unit_of(way, x, 1)))
            pl.when(s == (way + 1) * PIECES + FILL + 12)(lambda: add(unit_of(way, 1 - x, 0)))

    def finish():
        for way in WAYS:
            add(unit_of(way, 1 - x, 1))

    def drain():
        for way in WAYS:
            @pl.when(place.to_end(1 - way) < LAST)
            def _():
                def one(k, carry):
                    line_copy(way, k).wait_send()
                    return carry

                lax.fori_loop(0, HOPS, one, 0)

        def one(k, carry):
            for way in WAYS:
                forward_copy(way, k).wait_send()
            pl.when(place.is_end)(lambda: swap_copy(k).wait_send())
            return carry

        lax.fori_loop(0, PIECES, one, 0)

    return slot, finish, drain


def start_solve(gram, rest, right):
    i = lax.broadcasted_iota(jnp.int32, rest.shape, 0)
    j = lax.broadcasted_iota(jnp.int32, rest.shape, 1)
    rest[...] = gram[...]
    right[...] = jnp.where(i == j, 1.0, 0.0)


def solve_part(k, part, rest, right, inverse):
    size = rest.shape[0]
    block = size // PANELS
    lane = lax.broadcasted_iota(jnp.int32, (block, size), 1)
    line = lax.broadcasted_iota(jnp.int32, (block, size), 0)
    one_line = lax.broadcasted_iota(jnp.int32, (block, 1), 0)
    first = pl.multiple_of(k * block, block)
    lines = pl.ds(first, block)
    rows, side = rest[lines, :], right[lines, :]
    count = block // TURNS
    for start in range(part * count, (part + 1) * count, STEP):
        pivots = range(start, start + STEP)
        columns = [
            jnp.sum(jnp.where(lane == first + j, rows, 0.0), axis=1, keepdims=True)
            for j in pivots
        ]
        done = []
        for c, j in enumerate(pivots):
            column, later = columns[c], columns[c + 1 :]
            one = slice(j, j + 1)
            top, beside = rows[one, :], side[one, :]
            heads = [other[one, :] for other in later]
            for ratio, its_top, its_side, its_heads in done:
                e = len(its_heads) - len(later) - 1
                column = column - ratio * its_heads[e]
                top = top - ratio[one, :] * its_top
                beside = beside - ratio[one, :] * its_side
                heads = [
                    head - ratio[one, :] * its_heads[e + 1 + i]
                    for i, head in enumerate(heads)
                ]
            ratio = jnp.where(one_line > j, column * (1.0 / column[one, :]), 0.0)
            done.append((ratio, top, beside, heads))
        for ratio, top, beside, _ in done:
            rows = rows - ratio * top
            side = side - ratio * beside
    if part < TURNS - 1:
        rest[lines, :] = rows
        right[lines, :] = side
        return
    diagonal = jnp.sum(
        jnp.where(lane == first + line, rows, 0.0), axis=1, keepdims=True
    )
    scale = 1.0 / jnp.sqrt(diagonal)
    rows = jnp.where(lane >= first + line, rows * scale, 0.0)
    side = side * scale
    inverse[lines, :] = side
    rest[...] -= tn(rows, rows, HIGH)
    right[...] -= tn(rows, side, HIGH)


class Ring:
    def __init__(self, n):
        self.n, self.rows, self.cols = n, LINE, n // LINE
        self.body = self.rows * (self.cols - 1)
        self.tok = lax.axis_index("tok")
        self.pos = self.pos_of(self.tok)

    def pos_of(self, tok):
        r, c = lax.div(tok, self.cols), lax.rem(tok, self.cols)
        odd = lax.rem(r, 2)
        inner = lax.div(c + self.cols - 1, self.cols)
        along = r * (self.cols - 1) + (1 - odd) * (c - 1) + odd * (self.cols - 1 - c)
        back = self.body + self.rows - 1 - r
        return inner * along + (1 - inner) * back

    def tok_of(self, pos):
        last = lax.div(pos, self.body)
        r, k = lax.div(pos, self.cols - 1), lax.rem(pos, self.cols - 1)
        odd = lax.rem(r, 2)
        along = r * self.cols + (1 - odd) * (k + 1) + odd * (self.cols - 1 - k)
        back = (self.rows - 1 - (pos - self.body)) * self.cols
        return (1 - last) * along + last * back

    def at(self, offset):
        return lax.rem(self.pos + offset + 2 * self.n, self.n)

    def neighbours(self):
        return self.tok_of(self.at(1)), self.tok_of(self.at(-1))


def ring_scatter(ring, prepare, term, store, send, recv, sems):
    n = ring.n
    dest = ring.neighbours()

    def copy(way, step, piece):
        return remote(
            send.at[way, step, piece], recv.at[way, step, piece], sems, (way, step, piece),
            {"tok": dest[way]},
        )

    def block(way, step):
        return ring.at(-1 - step) if way == 0 else ring.at(1 + step)

    for piece in range(RING_PIECES):
        for way in WAYS:
            prepare(way, piece)
            send[way, 0, piece] = term(way, piece, block(way, 0)).astype(BF16)
            copy(way, 0, piece).start()

    def step(s, carry):
        for piece in range(RING_PIECES):
            for way in WAYS:
                own = term(way, piece, block(way, s))
                copy(way, s - 1, piece).wait_recv()
                total = own + recv[way, s - 1, piece].astype(F32)
                send[way, s, piece] = total.astype(BF16)
                copy(way, s, piece).start()
        return carry

    lax.fori_loop(1, n - 1, step, 0)
    for piece in range(RING_PIECES):
        for way in WAYS:
            own = term(way, piece, ring.pos)
            copy(way, n - 2, piece).wait_recv()
            store(way, piece, own + recv[way, n - 2, piece].astype(F32))

    def drain(s, carry):
        for piece in range(RING_PIECES):
            for way in WAYS:
                copy(way, s, piece).wait_send()
        return carry

    lax.fori_loop(0, n - 1, drain, 0)


def coeffs(place, proj, grads, out, terms, send, recv, sems, scale):
    ring = Ring(place.n)
    rows, width = out.shape
    part = width // (2 * RING_PIECES)

    def prepare(way, piece):
        first = (way * RING_PIECES + piece) * part
        last = first + part
        value = tn(proj[...], grads[:, first:last])
        terms[:, :, first:last] = (value * scale).reshape(place.n, rows, part)

    def term(way, piece, pos):
        first = (way * RING_PIECES + piece) * part
        return terms[ring.tok_of(pos), :, first : first + part]

    def store(way, piece, total):
        first = (way * RING_PIECES + piece) * part
        out[:, first : first + part] = total

    ring_scatter(ring, prepare, term, store, send, recv, sems)


def kernel(n, m, scale, names, acts_in, grads_in, test_in, out, *refs):
    s = types.SimpleNamespace(**dict(zip(names, refs)))
    place = Place(n, m)
    loads = [
        pltpu.make_async_copy(src, dst, s.load_sems.at[i])
        for i, (src, dst) in enumerate(
            ((grads_in, s.grads), (test_in, s.test), (acts_in, s.acts))
        )
    ]
    for load in loads:
        load.start()
    place.barrier()
    loads[0].wait()
    loads[1].wait()
    s.probe_part[...] = jnp.dot(s.grads[...], s.test[...], preferred_element_type=F32).T
    wid_sum(
        place, s.probe_part, s.probe_got, s.probe_mine, s.probe,
        (s.probe_send, s.probe_recv), lambda total: total,
    )
    loads[2].wait()
    reduce_slot, drain_reduce = reduce_sketch(
        place, s.acts, s.probe, s.terms, s.line, s.cross, s.last, s.full,
        (s.line_send, s.line_recv), (s.cross_send, s.cross_recv), (s.last_send, s.last_recv),
    )
    gram = Gram(
        place, s.gram_part, s.gram_got, s.gram_share, s.gram_cross, s.gram_ends,
        s.gram_mine, s.gram,
        (
            (s.gram_send, s.gram_recv), (s.gram_x_send, s.gram_x_recv),
            (s.gram_z_send, s.gram_z_recv),
        ),
    )
    gather_slot, finish_gather, drain_gather = gather_sketch(
        place, s.acts, s.full, s.mixed, gram, s.rest, s.right, s.inverse,
        (s.back_send, s.back_recv), (s.forward_send, s.forward_recv),
        (s.swap_send, s.swap_recv),
    )

    def slot(i, carry):
        reduce_slot(i)
        gather_slot(i - HOPS)
        return carry

    lax.fori_loop(0, SLOTS, slot, 0)
    finish_gather()
    wid_sum(
        place, s.mixed, s.mixed_got, s.proj_mine, s.proj, (s.mixed_send, s.mixed_recv),
        lambda total: nt(total, s.inverse[...], HIGH),
    )
    coeffs(
        place, s.proj, s.grads, out, s.out_terms, s.ring_from, s.ring_to,
        (s.ring_send, s.ring_recv), scale,
    )
    drain_reduce()
    drain_gather()
    gram.drain()


def scratch_of(n, m, tokens, hidden, rank, model):
    units = ENDS * 2 * PARTS
    block = (rank // PIECES, hidden // units)
    vmem, dma = pltpu.VMEM, pltpu.SemaphoreType.DMA
    rows = rank // n
    part = model // (2 * RING_PIECES)

    def pair(name, shape):
        return {name + "_send": dma(shape), name + "_recv": dma(shape)}

    return {
        "acts": vmem((tokens, hidden), BF16),
        "grads": vmem((tokens, model), BF16),
        "test": vmem((model, rank), BF16),
        "load_sems": dma((3,)),
        "probe_part": vmem((rank, tokens), F32),
        "probe_got": vmem((m - 1, rank // m, tokens), F32),
        "probe_mine": vmem((rank // m, tokens), BF16),
        "probe": vmem((rank, tokens), BF16),
        **pair("probe", (2, m - 1)),
        "terms": vmem((units, PIECES, *block), BF16),
        "line": vmem((ENDS, HOPS, *block), BF16),
        "cross": vmem((ENDS, PIECES, *block), BF16),
        "last": vmem((PIECES, *block), BF16),
        "full": vmem((units, PIECES, *block), BF16),
        **pair("line", (ENDS, HOPS)),
        **pair("cross", (ENDS, PIECES)),
        **pair("last", (PIECES,)),
        "gram_part": vmem((rank, rank), F32),
        "gram_got": vmem((m - 1, rank // m, rank), F32),
        "gram_share": vmem((rank // m, rank), F32),
        "gram_cross": vmem((rank // m, rank), F32),
        "gram_ends": vmem((ENDS, rank // m, rank), F32),
        "gram_mine": vmem((rank // m, rank), F32),
        "gram": vmem((rank, rank), F32),
        **pair("gram", (2, m - 1)),
        **pair("gram_x", (1,)),
        **pair("gram_z", (ENDS,)),
        "mixed": vmem((tokens, rank), F32),
        "rest": vmem((rank, rank), F32),
        "right": vmem((rank, rank), F32),
        "inverse": vmem((rank, rank), F32),
        **pair("back", (ENDS, HOPS)),
        **pair("forward", (ENDS, PIECES)),
        **pair("swap", (PIECES,)),
        "mixed_got": vmem((m - 1, tokens // m, rank), F32),
        "proj_mine": vmem((tokens // m, rank), BF16),
        "proj": vmem((tokens, rank), BF16),
        **pair("mixed", (2, m - 1)),
        "out_terms": vmem((n, rows, model), F32),
        "ring_from": vmem((2, n - 1, RING_PIECES, rows, part), BF16),
        "ring_to": vmem((2, n - 1, RING_PIECES, rows, part), BF16),
        **pair("ring", (2, n - 1, RING_PIECES)),
    }


def line_shards(n, m, acts, out_grads, test_matrix):
    tokens, hidden = acts.shape
    rank, model = test_matrix.shape[1], out_grads.shape[1]
    scratch = scratch_of(n, m, tokens, hidden, rank, model)
    scale = 1.0 / math.sqrt(tokens * n)
    return pl.pallas_call(
        functools.partial(kernel, n, m, scale, tuple(scratch)),
        out_shape=jax.ShapeDtypeStruct((rank // n, model), F32),
        in_specs=[pl.BlockSpec(memory_space=pl.ANY)] * 3,
        out_specs=pl.BlockSpec(memory_space=pltpu.VMEM),
        scratch_shapes=list(scratch.values()),
        compiler_params=pltpu.CompilerParams(
            collective_id=0, has_side_effects=True, vmem_limit_bytes=VMEM_LIMIT
        ),
    )(acts, out_grads, test_matrix)


def factor_inverse(gram):
    lower = jnp.linalg.cholesky(gram)
    eye_matrix = jnp.eye(gram.shape[0], dtype=F32)
    return lax.linalg.triangular_solve(lower, eye_matrix, left_side=True, lower=True)


def plain_shards(acts, out_grads, test_matrix):
    partial_probe = jnp.dot(out_grads, test_matrix, preferred_element_type=F32)
    probe = lax.psum(partial_probe, "wid").astype(BF16)
    local_sketch = lax.dot_general(
        acts, probe, (((0,), (0,)), ((), ())), preferred_element_type=F32
    )
    sketch = lax.psum(local_sketch.astype(BF16), "tok")
    gram = lax.psum(
        lax.dot_general(sketch, sketch, (((0,), (0,)), ((), ())), preferred_element_type=F32),
        "wid",
    )
    inverse = factor_inverse(gram)
    mixed = lax.psum(jnp.dot(acts, sketch, preferred_element_type=F32), "wid")
    proj = jnp.dot(mixed, inverse.T, precision=lax.Precision.HIGHEST).astype(BF16)
    scale = 1.0 / math.sqrt(acts.shape[0] * lax.axis_size("tok"))
    term = lax.dot_general(
        proj, out_grads, (((0,), (0,)), ((), ())), preferred_element_type=F32
    )
    return lax.psum_scatter(term * scale, "tok", scatter_dimension=0, tiled=True)


def solution(mesh):
    n, m = mesh.shape["tok"], mesh.shape["wid"]

    def shards(acts, out_grads, test_matrix):
        tokens, hidden = acts.shape
        model, rank = test_matrix.shape
        fits = (
            n == 2 * LINE
            and m > 1
            and tokens % (16 * m) == 0
            and rank % (16 * m) == 0
            and rank % (16 * PIECES) == 0
            and rank % (16 * n) == 0
            and rank % (PANELS * TURNS * STEP) == 0
            and hidden % (ENDS * 2 * PARTS * 128) == 0
            and model % (2 * RING_PIECES * 128) == 0
            and (tokens * hidden + 2 * rank * hidden) * 2 < VMEM_LIMIT // 2
        )
        if fits:
            return line_shards(n, m, acts, out_grads, test_matrix)
        return plain_shards(acts, out_grads, test_matrix)

    return jax.shard_map(
        shards,
        mesh=mesh,
        in_specs=(P("tok", "wid"), P("tok", "wid"), P("wid", None)),
        out_specs=P("tok", "wid"),
        check_vma=False,
    )
```

```python
import functools
import math
import types

import jax
import jax.numpy as jnp
from jax import lax
from jax.experimental import pallas as pl
from jax.experimental.pallas import tpu as pltpu
from jax.sharding import PartitionSpec as P

MESH = pl.DeviceIdType.MESH
F32 = jnp.float32
BF16 = jnp.bfloat16
HIGH = lax.Precision.HIGHEST
VMEM_LIMIT = 60 * 1024 * 1024
LINE = 4
ENDS = 2
PARTS = 2
PIECES = 16
PANELS = 8
TURNS = 2
STEP = 8
GROUPS = 3
HALVES = 2
SKEW = 5
HOPS = GROUPS * PIECES
LAST = LINE - 1
FILL = SKEW * LAST
REDUCED = HOPS + FILL
SLOTS = HOPS + REDUCED
WAYS = (0, 1)
RING_PIECES = 4


def nt(a, b, precision=None):
    return lax.dot_general(
        a, b, (((1,), (1,)), ((), ())), preferred_element_type=F32, precision=precision
    )


def tn(a, b, precision=None):
    return lax.dot_general(
        a, b, (((0,), (0,)), ((), ())), preferred_element_type=F32, precision=precision
    )


def both(a, b):
    return jnp.logical_and(a, b)


def within(value, first, count):
    return both(value >= first, value < first + count)


class Place:
    def __init__(self, n, m):
        self.n, self.m, self.cols = n, m, n // LINE
        self.tok, self.wid = lax.axis_index("tok"), lax.axis_index("wid")
        self.z, self.x = lax.div(self.tok, self.cols), lax.rem(self.tok, self.cols)
        self.across = self.z * self.cols + 1 - self.x
        self.end = lax.div(self.z, LAST)
        self.is_end = lax.rem(self.z, LAST) == 0

    def along(self, step):
        return lax.rem(self.z + step + LINE, LINE) * self.cols + self.x

    def to_end(self, end):
        return self.z if end else LAST - self.z

    def peer(self, k):
        return lax.rem(self.wid + k, self.m)

    def barrier(self):
        sem = pltpu.get_barrier_semaphore()
        others = [{"wid": self.peer(k)} for k in range(1, self.m)]
        others += [{"tok": self.along(step)} for step in range(1, LINE)]
        others += [{"tok": self.across}]
        for other in others:
            pl.semaphore_signal(sem, inc=1, device_id=other, device_id_type=MESH)
        pl.semaphore_wait(sem, len(others))


def remote(src, dst, sems, index, device):
    return pltpu.make_async_remote_copy(
        src_ref=src,
        dst_ref=dst,
        send_sem=sems[0].at[index],
        recv_sem=sems[1].at[index],
        device_id=device,
        device_id_type=MESH,
    )


def unit_of(end, x, part):
    return (end * 2 + x) * PARTS + part


def shares(place, rows):
    share = rows // place.m
    return lambda index: pl.ds(pl.multiple_of(index * share, 16), share)


def wid_sum(place, part, got, mine, out, sems, finish):
    lines = shares(place, part.shape[0])
    me = place.wid

    def copy(phase, k):
        other = place.peer(k)
        return remote(
            mine if phase else part.at[lines(other)],
            out.at[lines(me)] if phase else got.at[k - 1],
            sems,
            (phase, k - 1),
            {"wid": other},
        )

    for k in range(1, place.m):
        copy(0, k).start()
    total = part[lines(me), :]
    for k in range(1, place.m):
        copy(0, k).wait_recv()
        total = total + got[k - 1]
    total = finish(total).astype(mine.dtype)
    mine[...] = total
    for k in range(1, place.m):
        copy(1, k).start()
    out[lines(me), :] = total
    for k in range(1, place.m):
        copy(0, k).wait_send()
        copy(1, k).wait()


def reduce_sketch(place, acts, probe, terms, line, cross, last, full, line_sems, cross_sems, last_sems):
    x, end = place.x, place.end
    width = terms.shape[-1]

    def compute(unit):
        columns = pl.ds(pl.multiple_of(unit * width, 128), width)
        term = jnp.dot(probe[...], acts[:, columns], preferred_element_type=F32)
        terms[unit] = term.astype(BF16).reshape(terms.shape[1:])

    def order(i):
        side = jnp.where(lax.div(i, 4) == 0, 1 - x, x)
        k = lax.rem(i, 4)
        own = lax.div(k, 2)
        return unit_of(lax.rem(1 - end + own, 2), side, 1 - lax.rem(k, 2))

    def spot(end_, k):
        group, piece = lax.div(k, PIECES), lax.rem(k, PIECES)
        side = jnp.where(group == 0, 1 - x, x)
        part = jnp.where(group == GROUPS - 1, 0, 1)
        return group, piece, unit_of(end_, side, part)

    def line_copy(way, k, src):
        step = 1 if way else -1
        return remote(src, line.at[way, k], line_sems, (way, k), {"tok": place.along(step)})

    def cross_copy(way, piece):
        unit = unit_of(way, 1 - x, 0)
        return remote(
            terms.at[unit, piece], cross.at[way, piece], cross_sems, (way, piece),
            {"tok": place.across},
        )

    def last_copy(piece):
        return remote(
            line.at[end, piece], last.at[piece], last_sems, piece, {"tok": place.across}
        )

    def hop(way, k):
        pos = place.to_end(way)
        group, piece, unit = spot(way, k)

        @pl.when(pos == 0)
        def _():
            line_copy(way, k, terms.at[unit, piece]).start()

        @pl.when(pos > 0)
        def _():
            line_copy(way, k, line.at[way, k]).wait_recv()

        @pl.when(both(pos > 0, group != 1))
        def _():
            total = line[way, k].astype(F32) + terms[unit, piece].astype(F32)
            line[way, k] = total.astype(BF16)

        @pl.when(both(both(pos > 0, pos < LAST), group == 1))
        def _():
            total = line[way, k].astype(F32) + terms[unit, piece].astype(F32)
            line[way, k] = total.astype(BF16)

        @pl.when(both(pos > 0, pos < LAST))
        def _():
            line_copy(way, k, line.at[way, k]).start()

        @pl.when(both(pos == LAST, group == GROUPS - 1))
        def _():
            full[unit, piece] = line[way, k]

    compute(order(0))

    def slot(s):
        for way in WAYS:
            k = s - SKEW * place.to_end(way)
            pl.when(within(k, 0, HOPS))(functools.partial(hop, way, k))

        pl.when(within(s, 0, 7))(lambda: compute(order(s + 1)))

        @pl.when(s < 2 * PIECES)
        def _():
            first = lax.rem(1 - end + lax.div(s, PIECES), 2)
            cross_copy(first, lax.rem(s, PIECES)).start()

        @pl.when(within(s, 2 * PIECES - 2, PIECES))
        def _():
            piece = s - (2 * PIECES - 2)
            for way in WAYS:
                cross_copy(way, piece).wait_recv()
                unit = unit_of(way, x, 0)
                total = terms[unit, piece].astype(F32) + cross[way, piece].astype(F32)
                terms[unit, piece] = total.astype(BF16)

        @pl.when(both(place.is_end, within(s, 2 * PIECES - 3, PIECES)))
        def _():
            last_copy(s - (2 * PIECES - 3)).start()

        @pl.when(both(place.is_end, within(s, REDUCED - PIECES, PIECES)))
        def _():
            piece = s - (REDUCED - PIECES)
            last_copy(piece).wait_recv()
            unit = unit_of(end, x, 1)
            total = line[end, PIECES + piece].astype(F32) + last[piece].astype(F32)
            total = total + terms[unit, piece].astype(F32)
            full[unit, piece] = total.astype(BF16)

    def drain():
        for way in WAYS:
            sent = place.to_end(way) < LAST

            @pl.when(sent)
            def _():
                def one(k, carry):
                    line_copy(way, k, line.at[way, k]).wait_send()
                    return carry

                lax.fori_loop(0, HOPS, one, 0)

        def one(k, carry):
            for way in WAYS:
                cross_copy(way, k).wait_send()
            pl.when(place.is_end)(lambda: last_copy(k).wait_send())
            return carry

        lax.fori_loop(0, PIECES, one, 0)

    return slot, drain


class Projections:
    def __init__(self, place, mixed, got, totals, mine, proj, inverse, sems):
        self.place, self.mixed, self.got, self.totals = place, mixed, got, totals
        self.mine, self.proj, self.inverse, self.sems = mine, proj, inverse, sems
        self.lines = shares(place, mixed.shape[1])
        self.peers = range(1, place.m)

    def first(self, half, k):
        other = self.place.peer(k)
        return remote(
            self.mixed.at[half, self.lines(other)], self.got.at[half, k - 1], self.sems,
            (0, half, k - 1), {"wid": other},
        )

    def second(self, half, k):
        return remote(
            self.mine.at[half], self.proj.at[half, self.lines(self.place.wid)], self.sems,
            (1, half, k - 1), {"wid": self.place.peer(k)},
        )

    def start(self, half):
        for k in self.peers:
            self.first(half, k).start()

    def spread(self, half):
        total = self.mixed[half, self.lines(self.place.wid), :]
        for k in self.peers:
            self.first(half, k).wait_recv()
            total = total + self.got[half, k - 1]
        self.totals[half] = total
        size = total.shape[1]
        lines = slice(half * size, (half + 1) * size)
        value = jnp.zeros_like(total)
        for h in range(half + 1):
            block = self.inverse[lines, h * size : (h + 1) * size]
            value = value + nt(self.totals[h], block, HIGH)
        value = value.astype(self.mine.dtype)
        self.mine[half] = value
        for k in self.peers:
            self.second(half, k).start()
        self.proj[half, self.lines(self.place.wid), :] = value

    def finish(self):
        for half in range(HALVES):
            for k in self.peers:
                self.second(half, k).wait_recv()

    def drain(self):
        for half in range(HALVES):
            for k in self.peers:
                self.first(half, k).wait_send()
                self.second(half, k).wait_send()


class Gram:
    def __init__(self, place, part, got, share, crossed, ends, mine, gram, sems):
        self.place, self.part, self.got, self.share = place, part, got, share
        self.crossed, self.ends, self.mine, self.gram = crossed, ends, mine, gram
        self.wid_sems, self.cross_sems, self.end_sems = sems
        self.lines = shares(place, gram.shape[0])

    def first(self, k):
        other = self.place.peer(k)
        return remote(
            self.part.at[self.lines(other)], self.got.at[k - 1], self.wid_sems, (0, k - 1),
            {"wid": other},
        )

    def over_x(self):
        return remote(
            self.share, self.crossed, self.cross_sems, 0, {"tok": self.place.across}
        )

    def over_z(self, end):
        block = self.ends.at[end]
        step = -1 if end else 1
        return remote(block, block, self.end_sems, end, {"tok": self.place.along(step)})

    def spread(self, k):
        return remote(
            self.mine, self.gram.at[self.lines(self.place.wid)], self.wid_sems, (1, k - 1),
            {"wid": self.place.peer(k)},
        )

    def start(self, full):
        @pl.when(self.place.is_end)
        def _():
            rank, width = self.part.shape[0], full.shape[-1]
            unit = unit_of(self.place.end, self.place.x, 0)
            a = full[unit].reshape(rank, width)
            b = full[unit + 1].reshape(rank, width)
            self.part[...] = nt(a, a) + nt(b, b)
            for k in range(1, self.place.m):
                self.first(k).start()

    def cross(self):
        @pl.when(self.place.is_end)
        def _():
            total = self.part[self.lines(self.place.wid), :]
            for k in range(1, self.place.m):
                self.first(k).wait_recv()
                total = total + self.got[k - 1]
            self.share[...] = total
            self.over_x().start()

    def along(self):
        @pl.when(self.place.is_end)
        def _():
            self.over_x().wait_recv()
            self.ends[self.place.end] = self.share[...] + self.crossed[...]
            for end in range(ENDS):
                pl.when(self.place.end == end)(lambda: self.over_z(end).start())

    def relay(self, step):
        for end in range(ENDS):
            @pl.when(self.place.to_end(1 - end) == step)
            def _():
                self.over_z(end).wait_recv()
                if step < LAST:
                    self.over_z(end).start()

    def gather(self):
        self.relay(LAST)
        total = self.ends[0] + self.ends[1]
        self.mine[...] = total
        for k in range(1, self.place.m):
            self.spread(k).start()
        self.gram[self.lines(self.place.wid), :] = total

    def finish(self):
        for k in range(1, self.place.m):
            self.spread(k).wait_recv()

    def drain(self):
        @pl.when(self.place.is_end)
        def _():
            for k in range(1, self.place.m):
                self.first(k).wait_send()
            self.over_x().wait_send()

        for end in range(ENDS):
            pl.when(self.place.to_end(1 - end) < LAST)(
                lambda: self.over_z(end).wait_send()
            )
        for k in range(1, self.place.m):
            self.spread(k).wait_send()


def gather_sketch(place, acts, full, sums, gram, rest, right, inverse, line_sems, forward_sems, swap_sems):
    x, end = place.x, place.end
    rank, width = rest.shape[0], full.shape[-1]
    mixed, run = sums.mixed, PIECES // HALVES
    per_half = GROUPS * run
    solve_at = FILL + 29

    def spot(end_, k):
        half, rest_of = lax.div(k, per_half), lax.rem(k, per_half)
        group, piece = lax.div(rest_of, run), half * run + lax.rem(rest_of, run)
        side = jnp.where(group == GROUPS - 1, 1 - x, x)
        part = jnp.where(group == 0, 0, 1)
        return group, piece, unit_of(end_, side, part)

    def copy(unit, piece, sems, index, device):
        block = full.at[unit, piece]
        return remote(block, block, sems, index, {"tok": device})

    def line_copy(way, k):
        group, piece, unit = spot(way, k)
        return copy(unit, piece, line_sems, (way, k), place.along(-1 if way else 1))

    def forward_copy(way, piece):
        return copy(unit_of(way, x, 0), piece, forward_sems, (way, piece), place.across)

    def swap_copy(piece):
        return copy(unit_of(end, x, 1), piece, swap_sems, piece, place.across)

    def hop(way, k):
        pos = place.to_end(1 - way)
        group, piece, unit = spot(way, k)

        @pl.when(pos > 0)
        def _():
            line_copy(way, k).wait_recv()

        @pl.when(both(pos == 0, group == GROUPS - 1))
        def _():
            swap_copy(piece).wait_recv()

        @pl.when(pos < LAST)
        def _():
            line_copy(way, k).start()

    def add(half, unit):
        columns = pl.ds(pl.multiple_of(unit * width, 128), width)
        block = full[unit, half * run : (half + 1) * run]
        mixed[half] += nt(acts[:, columns], block.reshape(rank // HALVES, width))

    adds = []
    for half in range(HALVES):
        for way in WAYS:
            ready = half * per_half + FILL + way
            adds.append((ready + run, half, unit_of(way, x, 0)))
            adds.append((ready + 2 * run, half, unit_of(way, x, 1)))
            adds.append((ready + 3 * run, half, unit_of(way, 1 - x, 1)))
            adds.append((ready + (way + 2) * run + 2, half, unit_of(way, 1 - x, 0)))

    mixed[...] = jnp.zeros_like(mixed)

    def slot(s):
        @pl.when(both(place.is_end, within(s, 0, PIECES)))
        def _():
            swap_copy(s).start()

        for way in WAYS:
            k = s - SKEW * place.to_end(1 - way)
            pl.when(within(k, 0, HOPS))(functools.partial(hop, way, k))
            for half in range(HALVES):
                sent = s - FILL - half * per_half - way * run
                piece = half * run + sent
                pl.when(within(sent, 0, run))(lambda: forward_copy(way, piece).start())
                pl.when(within(sent, run, run))(
                    lambda: forward_copy(way, piece - run).wait_recv()
                )

        pl.when(s == FILL)(lambda: gram.start(full))
        pl.when(s == FILL + 4)(gram.cross)
        pl.when(s == FILL + 9)(gram.along)
        for step in range(1, LAST):
            pl.when(s == FILL + 9 + 5 * step)(lambda: gram.relay(step))
        pl.when(s == FILL + 9 + 5 * LAST)(gram.gather)

        @pl.when(s == solve_at - 1)
        def _():
            gram.finish()
            start_solve(gram.gram, rest, right)

        solve = s - solve_at
        for part in range(TURNS):
            mine = both(within(solve, 0, TURNS * PANELS), lax.rem(solve, TURNS) == part)
            pl.when(mine)(
                lambda: solve_part(lax.div(solve, TURNS), part, rest, right, inverse)
            )

        for at, half, unit in adds:
            if at < HOPS + FILL:
                pl.when(s == at)(lambda: add(half, unit))
        pl.when(s == FILL + per_half + 4)(lambda: sums.start(0))
        pl.when(s == solve_at + TURNS * PANELS // HALVES + 2)(lambda: sums.spread(0))

    def finish():
        for at, half, unit in adds:
            if at >= HOPS + FILL:
                add(half, unit)
        sums.start(1)
        sums.spread(1)
        sums.finish()

    def drain():
        for way in WAYS:
            @pl.when(place.to_end(1 - way) < LAST)
            def _():
                def one(k, carry):
                    line_copy(way, k).wait_send()
                    return carry

                lax.fori_loop(0, HOPS, one, 0)

        def one(k, carry):
            for way in WAYS:
                forward_copy(way, k).wait_send()
            pl.when(place.is_end)(lambda: swap_copy(k).wait_send())
            return carry

        lax.fori_loop(0, PIECES, one, 0)

    return slot, finish, drain


def start_solve(gram, rest, right):
    i = lax.broadcasted_iota(jnp.int32, rest.shape, 0)
    j = lax.broadcasted_iota(jnp.int32, rest.shape, 1)
    rest[...] = gram[...]
    right[...] = jnp.where(i == j, 1.0, 0.0)


def solve_part(k, part, rest, right, inverse):
    size = rest.shape[0]
    block = size // PANELS
    lane = lax.broadcasted_iota(jnp.int32, (block, size), 1)
    line = lax.broadcasted_iota(jnp.int32, (block, size), 0)
    one_line = lax.broadcasted_iota(jnp.int32, (block, 1), 0)
    first = pl.multiple_of(k * block, block)
    lines = pl.ds(first, block)
    rows, side = rest[lines, :], right[lines, :]
    count = block // TURNS
    for start in range(part * count, (part + 1) * count, STEP):
        pivots = range(start, start + STEP)
        columns = [
            jnp.sum(jnp.where(lane == first + j, rows, 0.0), axis=1, keepdims=True)
            for j in pivots
        ]
        done = []
        for c, j in enumerate(pivots):
            column, later = columns[c], columns[c + 1 :]
            one = slice(j, j + 1)
            top, beside = rows[one, :], side[one, :]
            heads = [other[one, :] for other in later]
            for ratio, its_top, its_side, its_heads in done:
                e = len(its_heads) - len(later) - 1
                column = column - ratio * its_heads[e]
                top = top - ratio[one, :] * its_top
                beside = beside - ratio[one, :] * its_side
                heads = [
                    head - ratio[one, :] * its_heads[e + 1 + i]
                    for i, head in enumerate(heads)
                ]
            ratio = jnp.where(one_line > j, column * (1.0 / column[one, :]), 0.0)
            done.append((ratio, top, beside, heads))
        for ratio, top, beside, _ in done:
            rows = rows - ratio * top
            side = side - ratio * beside
    if part < TURNS - 1:
        rest[lines, :] = rows
        right[lines, :] = side
        return
    diagonal = jnp.sum(
        jnp.where(lane == first + line, rows, 0.0), axis=1, keepdims=True
    )
    scale = 1.0 / jnp.sqrt(diagonal)
    rows = jnp.where(lane >= first + line, rows * scale, 0.0)
    side = side * scale
    inverse[lines, :] = side
    rest[...] -= tn(rows, rows, HIGH)
    right[...] -= tn(rows, side, HIGH)


class Ring:
    def __init__(self, n):
        self.n, self.rows, self.cols = n, LINE, n // LINE
        self.body = self.rows * (self.cols - 1)
        self.tok = lax.axis_index("tok")
        self.pos = self.pos_of(self.tok)

    def pos_of(self, tok):
        r, c = lax.div(tok, self.cols), lax.rem(tok, self.cols)
        odd = lax.rem(r, 2)
        inner = lax.div(c + self.cols - 1, self.cols)
        along = r * (self.cols - 1) + (1 - odd) * (c - 1) + odd * (self.cols - 1 - c)
        back = self.body + self.rows - 1 - r
        return inner * along + (1 - inner) * back

    def tok_of(self, pos):
        last = lax.div(pos, self.body)
        r, k = lax.div(pos, self.cols - 1), lax.rem(pos, self.cols - 1)
        odd = lax.rem(r, 2)
        along = r * self.cols + (1 - odd) * (k + 1) + odd * (self.cols - 1 - k)
        back = (self.rows - 1 - (pos - self.body)) * self.cols
        return (1 - last) * along + last * back

    def at(self, offset):
        return lax.rem(self.pos + offset + 2 * self.n, self.n)

    def neighbours(self):
        return self.tok_of(self.at(1)), self.tok_of(self.at(-1))


def ring_scatter(ring, prepare, term, store, send, recv, sems):
    n = ring.n
    dest = ring.neighbours()

    def copy(way, step, piece):
        return remote(
            send.at[way, step, piece], recv.at[way, step, piece], sems, (way, step, piece),
            {"tok": dest[way]},
        )

    def block(way, step):
        return ring.at(-1 - step) if way == 0 else ring.at(1 + step)

    for piece in range(RING_PIECES):
        for way in WAYS:
            prepare(way, piece)
            send[way, 0, piece] = term(way, piece, block(way, 0)).astype(BF16)
            copy(way, 0, piece).start()

    def step(s, carry):
        for piece in range(RING_PIECES):
            for way in WAYS:
                own = term(way, piece, block(way, s))
                copy(way, s - 1, piece).wait_recv()
                total = own + recv[way, s - 1, piece].astype(F32)
                send[way, s, piece] = total.astype(BF16)
                copy(way, s, piece).start()
        return carry

    lax.fori_loop(1, n - 1, step, 0)
    for piece in range(RING_PIECES):
        for way in WAYS:
            own = term(way, piece, ring.pos)
            copy(way, n - 2, piece).wait_recv()
            store(way, piece, own + recv[way, n - 2, piece].astype(F32))

    def drain(s, carry):
        for piece in range(RING_PIECES):
            for way in WAYS:
                copy(way, s, piece).wait_send()
        return carry

    lax.fori_loop(0, n - 1, drain, 0)


def coeffs(place, proj, grads, out, terms, send, recv, sems, scale):
    ring = Ring(place.n)
    rows, width = out.shape
    part = width // (2 * RING_PIECES)

    def prepare(way, piece):
        first = (way * RING_PIECES + piece) * part
        last = first + part
        count = place.n // HALVES
        for half in range(HALVES):
            value = tn(proj[half], grads[:, first:last])
            blocks = slice(half * count, (half + 1) * count)
            terms[blocks, :, first:last] = (value * scale).reshape(count, rows, part)

    def term(way, piece, pos):
        first = (way * RING_PIECES + piece) * part
        return terms[ring.tok_of(pos), :, first : first + part]

    def store(way, piece, total):
        first = (way * RING_PIECES + piece) * part
        out[:, first : first + part] = total

    ring_scatter(ring, prepare, term, store, send, recv, sems)


def kernel(n, m, scale, names, acts_in, grads_in, test_in, out, *refs):
    s = types.SimpleNamespace(**dict(zip(names, refs)))
    place = Place(n, m)
    loads = [
        pltpu.make_async_copy(src, dst, s.load_sems.at[i])
        for i, (src, dst) in enumerate(
            ((grads_in, s.grads), (test_in, s.test), (acts_in, s.acts))
        )
    ]
    for load in loads:
        load.start()
    place.barrier()
    loads[0].wait()
    loads[1].wait()
    s.probe_part[...] = jnp.dot(s.grads[...], s.test[...], preferred_element_type=F32).T
    wid_sum(
        place, s.probe_part, s.probe_got, s.probe_mine, s.probe,
        (s.probe_send, s.probe_recv), lambda total: total,
    )
    loads[2].wait()
    reduce_slot, drain_reduce = reduce_sketch(
        place, s.acts, s.probe, s.terms, s.line, s.cross, s.last, s.full,
        (s.line_send, s.line_recv), (s.cross_send, s.cross_recv), (s.last_send, s.last_recv),
    )
    gram = Gram(
        place, s.gram_part, s.gram_got, s.gram_share, s.gram_cross, s.gram_ends,
        s.gram_mine, s.gram,
        (
            (s.gram_send, s.gram_recv), (s.gram_x_send, s.gram_x_recv),
            (s.gram_z_send, s.gram_z_recv),
        ),
    )
    sums = Projections(
        place, s.mixed, s.mixed_got, s.mixed_totals, s.proj_mine, s.proj, s.inverse,
        (s.mixed_send, s.mixed_recv),
    )
    gather_slot, finish_gather, drain_gather = gather_sketch(
        place, s.acts, s.full, sums, gram, s.rest, s.right, s.inverse,
        (s.back_send, s.back_recv), (s.forward_send, s.forward_recv),
        (s.swap_send, s.swap_recv),
    )

    def slot(i, carry):
        reduce_slot(i)
        gather_slot(i - HOPS)
        return carry

    lax.fori_loop(0, SLOTS, slot, 0)
    finish_gather()
    coeffs(
        place, s.proj, s.grads, out, s.out_terms, s.ring_from, s.ring_to,
        (s.ring_send, s.ring_recv), scale,
    )
    drain_reduce()
    drain_gather()
    gram.drain()
    sums.drain()


def scratch_of(n, m, tokens, hidden, rank, model):
    units = ENDS * 2 * PARTS
    block = (rank // PIECES, hidden // units)
    vmem, dma = pltpu.VMEM, pltpu.SemaphoreType.DMA
    rows = rank // n
    part = model // (2 * RING_PIECES)

    def pair(name, shape):
        return {name + "_send": dma(shape), name + "_recv": dma(shape)}

    return {
        "acts": vmem((tokens, hidden), BF16),
        "grads": vmem((tokens, model), BF16),
        "test": vmem((model, rank), BF16),
        "load_sems": dma((3,)),
        "probe_part": vmem((rank, tokens), F32),
        "probe_got": vmem((m - 1, rank // m, tokens), F32),
        "probe_mine": vmem((rank // m, tokens), BF16),
        "probe": vmem((rank, tokens), BF16),
        **pair("probe", (2, m - 1)),
        "terms": vmem((units, PIECES, *block), BF16),
        "line": vmem((ENDS, HOPS, *block), BF16),
        "cross": vmem((ENDS, PIECES, *block), BF16),
        "last": vmem((PIECES, *block), BF16),
        "full": vmem((units, PIECES, *block), BF16),
        **pair("line", (ENDS, HOPS)),
        **pair("cross", (ENDS, PIECES)),
        **pair("last", (PIECES,)),
        "gram_part": vmem((rank, rank), F32),
        "gram_got": vmem((m - 1, rank // m, rank), F32),
        "gram_share": vmem((rank // m, rank), F32),
        "gram_cross": vmem((rank // m, rank), F32),
        "gram_ends": vmem((ENDS, rank // m, rank), F32),
        "gram_mine": vmem((rank // m, rank), F32),
        "gram": vmem((rank, rank), F32),
        **pair("gram", (2, m - 1)),
        **pair("gram_x", (1,)),
        **pair("gram_z", (ENDS,)),
        "mixed": vmem((HALVES, tokens, rank // HALVES), F32),
        "rest": vmem((rank, rank), F32),
        "right": vmem((rank, rank), F32),
        "inverse": vmem((rank, rank), F32),
        **pair("back", (ENDS, HOPS)),
        **pair("forward", (ENDS, PIECES)),
        **pair("swap", (PIECES,)),
        "mixed_got": vmem((HALVES, m - 1, tokens // m, rank // HALVES), F32),
        "mixed_totals": vmem((HALVES, tokens // m, rank // HALVES), F32),
        "proj_mine": vmem((HALVES, tokens // m, rank // HALVES), BF16),
        "proj": vmem((HALVES, tokens, rank // HALVES), BF16),
        **pair("mixed", (2, HALVES, m - 1)),
        "out_terms": vmem((n, rows, model), F32),
        "ring_from": vmem((2, n - 1, RING_PIECES, rows, part), BF16),
        "ring_to": vmem((2, n - 1, RING_PIECES, rows, part), BF16),
        **pair("ring", (2, n - 1, RING_PIECES)),
    }


def line_shards(n, m, acts, out_grads, test_matrix):
    tokens, hidden = acts.shape
    rank, model = test_matrix.shape[1], out_grads.shape[1]
    scratch = scratch_of(n, m, tokens, hidden, rank, model)
    scale = 1.0 / math.sqrt(tokens * n)
    return pl.pallas_call(
        functools.partial(kernel, n, m, scale, tuple(scratch)),
        out_shape=jax.ShapeDtypeStruct((rank // n, model), F32),
        in_specs=[pl.BlockSpec(memory_space=pl.ANY)] * 3,
        out_specs=pl.BlockSpec(memory_space=pltpu.VMEM),
        scratch_shapes=list(scratch.values()),
        compiler_params=pltpu.CompilerParams(
            collective_id=0, has_side_effects=True, vmem_limit_bytes=VMEM_LIMIT
        ),
    )(acts, out_grads, test_matrix)


def factor_inverse(gram):
    lower = jnp.linalg.cholesky(gram)
    eye_matrix = jnp.eye(gram.shape[0], dtype=F32)
    return lax.linalg.triangular_solve(lower, eye_matrix, left_side=True, lower=True)


def plain_shards(acts, out_grads, test_matrix):
    partial_probe = jnp.dot(out_grads, test_matrix, preferred_element_type=F32)
    probe = lax.psum(partial_probe, "wid").astype(BF16)
    local_sketch = lax.dot_general(
        acts, probe, (((0,), (0,)), ((), ())), preferred_element_type=F32
    )
    sketch = lax.psum(local_sketch.astype(BF16), "tok")
    gram = lax.psum(
        lax.dot_general(sketch, sketch, (((0,), (0,)), ((), ())), preferred_element_type=F32),
        "wid",
    )
    inverse = factor_inverse(gram)
    mixed = lax.psum(jnp.dot(acts, sketch, preferred_element_type=F32), "wid")
    proj = jnp.dot(mixed, inverse.T, precision=lax.Precision.HIGHEST).astype(BF16)
    scale = 1.0 / math.sqrt(acts.shape[0] * lax.axis_size("tok"))
    term = lax.dot_general(
        proj, out_grads, (((0,), (0,)), ((), ())), preferred_element_type=F32
    )
    return lax.psum_scatter(term * scale, "tok", scatter_dimension=0, tiled=True)


def solution(mesh):
    n, m = mesh.shape["tok"], mesh.shape["wid"]

    def shards(acts, out_grads, test_matrix):
        tokens, hidden = acts.shape
        model, rank = test_matrix.shape
        fits = (
            n == 2 * LINE
            and m > 1
            and tokens % (16 * m) == 0
            and rank % (16 * m) == 0
            and rank % (16 * PIECES) == 0
            and rank % (16 * n) == 0
            and rank % (PANELS * TURNS * STEP) == 0
            and rank % (HALVES * 128) == 0
            and hidden % (ENDS * 2 * PARTS * 128) == 0
            and model % (2 * RING_PIECES * 128) == 0
            and (tokens * hidden + 2 * rank * hidden) * 2 < VMEM_LIMIT // 2
        )
        if fits:
            return line_shards(n, m, acts, out_grads, test_matrix)
        return plain_shards(acts, out_grads, test_matrix)

    return jax.shard_map(
        shards,
        mesh=mesh,
        in_specs=(P("tok", "wid"), P("tok", "wid"), P("wid", None)),
        out_specs=P("tok", "wid"),
        check_vma=False,
    )
```

```python
import functools
import math
import types

import jax
import jax.numpy as jnp
from jax import lax
from jax.experimental import pallas as pl
from jax.experimental.pallas import tpu as pltpu
from jax.sharding import PartitionSpec as P

MESH = pl.DeviceIdType.MESH
F32 = jnp.float32
BF16 = jnp.bfloat16
HIGH = lax.Precision.HIGHEST
VMEM_LIMIT = 60 * 1024 * 1024
LINE = 4
ENDS = 2
PARTS = 2
PIECES = 16
PANELS = 8
TURNS = 2
STEP = 8
GROUPS = 3
HALVES = 2
SKEW = 5
HOPS = GROUPS * PIECES
LAST = LINE - 1
FILL = SKEW * LAST
REDUCED = HOPS + FILL
SLOTS = HOPS + REDUCED
WAYS = (0, 1)
RING_PIECES = 4


def nt(a, b, precision=None):
    return lax.dot_general(
        a, b, (((1,), (1,)), ((), ())), preferred_element_type=F32, precision=precision
    )


def tn(a, b, precision=None):
    return lax.dot_general(
        a, b, (((0,), (0,)), ((), ())), preferred_element_type=F32, precision=precision
    )


def both(a, b):
    return jnp.logical_and(a, b)


def within(value, first, count):
    return both(value >= first, value < first + count)


class Place:
    def __init__(self, n, m):
        self.n, self.m, self.cols = n, m, n // LINE
        self.tok, self.wid = lax.axis_index("tok"), lax.axis_index("wid")
        self.z, self.x = lax.div(self.tok, self.cols), lax.rem(self.tok, self.cols)
        self.across = self.z * self.cols + 1 - self.x
        self.end = lax.div(self.z, LAST)
        self.is_end = lax.rem(self.z, LAST) == 0

    def along(self, step):
        return lax.rem(self.z + step + LINE, LINE) * self.cols + self.x

    def to_end(self, end):
        return self.z if end else LAST - self.z

    def peer(self, k):
        return lax.rem(self.wid + k, self.m)

    def barrier(self):
        sem = pltpu.get_barrier_semaphore()
        others = [{"wid": self.peer(k)} for k in range(1, self.m)]
        others += [{"tok": self.along(step)} for step in range(1, LINE)]
        others += [{"tok": self.across}]
        for other in others:
            pl.semaphore_signal(sem, inc=1, device_id=other, device_id_type=MESH)
        pl.semaphore_wait(sem, len(others))


def remote(src, dst, sems, index, device):
    return pltpu.make_async_remote_copy(
        src_ref=src,
        dst_ref=dst,
        send_sem=sems[0].at[index],
        recv_sem=sems[1].at[index],
        device_id=device,
        device_id_type=MESH,
    )


def unit_of(end, x, part):
    return (end * 2 + x) * PARTS + part


def shares(place, rows):
    share = rows // place.m
    return lambda index: pl.ds(pl.multiple_of(index * share, 16), share)


def wid_sum(place, part, got, mine, out, sems, finish):
    lines = shares(place, part.shape[0])
    me = place.wid

    def copy(phase, k):
        other = place.peer(k)
        return remote(
            mine if phase else part.at[lines(other)],
            out.at[lines(me)] if phase else got.at[k - 1],
            sems,
            (phase, k - 1),
            {"wid": other},
        )

    for k in range(1, place.m):
        copy(0, k).start()
    total = part[lines(me), :]
    for k in range(1, place.m):
        copy(0, k).wait_recv()
        total = total + got[k - 1]
    total = finish(total).astype(mine.dtype)
    mine[...] = total
    for k in range(1, place.m):
        copy(1, k).start()
    out[lines(me), :] = total
    for k in range(1, place.m):
        copy(0, k).wait_send()
        copy(1, k).wait()


def reduce_sketch(place, acts, probe, terms, line, cross, last, full, line_sems, cross_sems, last_sems):
    x, end = place.x, place.end
    width = terms.shape[-1]

    def compute(unit):
        columns = pl.ds(pl.multiple_of(unit * width, 128), width)
        term = jnp.dot(probe[...], acts[:, columns], preferred_element_type=F32)
        terms[unit] = term.astype(BF16).reshape(terms.shape[1:])

    def order(i):
        side = jnp.where(lax.div(i, 4) == 0, 1 - x, x)
        k = lax.rem(i, 4)
        own = lax.div(k, 2)
        return unit_of(lax.rem(1 - end + own, 2), side, 1 - lax.rem(k, 2))

    def spot(end_, k):
        group, piece = lax.div(k, PIECES), lax.rem(k, PIECES)
        side = jnp.where(group == 0, 1 - x, x)
        part = jnp.where(group == GROUPS - 1, 0, 1)
        return group, piece, unit_of(end_, side, part)

    def line_copy(way, k, src):
        step = 1 if way else -1
        return remote(src, line.at[way, k], line_sems, (way, k), {"tok": place.along(step)})

    def cross_copy(way, piece):
        unit = unit_of(way, 1 - x, 0)
        return remote(
            terms.at[unit, piece], cross.at[way, piece], cross_sems, (way, piece),
            {"tok": place.across},
        )

    def last_copy(piece):
        return remote(
            line.at[end, piece], last.at[piece], last_sems, piece, {"tok": place.across}
        )

    def hop(way, k):
        pos = place.to_end(way)
        group, piece, unit = spot(way, k)

        @pl.when(pos == 0)
        def _():
            line_copy(way, k, terms.at[unit, piece]).start()

        @pl.when(pos > 0)
        def _():
            line_copy(way, k, line.at[way, k]).wait_recv()

        @pl.when(both(pos > 0, group != 1))
        def _():
            total = line[way, k].astype(F32) + terms[unit, piece].astype(F32)
            line[way, k] = total.astype(BF16)

        @pl.when(both(both(pos > 0, pos < LAST), group == 1))
        def _():
            total = line[way, k].astype(F32) + terms[unit, piece].astype(F32)
            line[way, k] = total.astype(BF16)

        @pl.when(both(pos > 0, pos < LAST))
        def _():
            line_copy(way, k, line.at[way, k]).start()

        @pl.when(both(pos == LAST, group == GROUPS - 1))
        def _():
            full[unit, piece] = line[way, k]

    compute(order(0))

    def slot(s):
        for way in WAYS:
            k = s - SKEW * place.to_end(way)
            pl.when(within(k, 0, HOPS))(functools.partial(hop, way, k))

        pl.when(within(s, 0, 7))(lambda: compute(order(s + 1)))

        @pl.when(s < 2 * PIECES)
        def _():
            first = lax.rem(1 - end + lax.div(s, PIECES), 2)
            cross_copy(first, lax.rem(s, PIECES)).start()

        @pl.when(within(s, 2 * PIECES - 2, PIECES))
        def _():
            piece = s - (2 * PIECES - 2)
            for way in WAYS:
                cross_copy(way, piece).wait_recv()
                unit = unit_of(way, x, 0)
                total = terms[unit, piece].astype(F32) + cross[way, piece].astype(F32)
                terms[unit, piece] = total.astype(BF16)

        @pl.when(both(place.is_end, within(s, 2 * PIECES - 3, PIECES)))
        def _():
            last_copy(s - (2 * PIECES - 3)).start()

        @pl.when(both(place.is_end, within(s, REDUCED - PIECES, PIECES)))
        def _():
            piece = s - (REDUCED - PIECES)
            last_copy(piece).wait_recv()
            unit = unit_of(end, x, 1)
            total = line[end, PIECES + piece].astype(F32) + last[piece].astype(F32)
            total = total + terms[unit, piece].astype(F32)
            full[unit, piece] = total.astype(BF16)

    def drain():
        for way in WAYS:
            sent = place.to_end(way) < LAST

            @pl.when(sent)
            def _():
                def one(k, carry):
                    line_copy(way, k, line.at[way, k]).wait_send()
                    return carry

                lax.fori_loop(0, HOPS, one, 0)

        def one(k, carry):
            for way in WAYS:
                cross_copy(way, k).wait_send()
            pl.when(place.is_end)(lambda: last_copy(k).wait_send())
            return carry

        lax.fori_loop(0, PIECES, one, 0)

    return slot, drain


class Projections:
    def __init__(self, place, mixed, got, totals, mine, proj, inverse, sems):
        self.place, self.mixed, self.got, self.totals = place, mixed, got, totals
        self.mine, self.proj, self.inverse, self.sems = mine, proj, inverse, sems
        self.lines = shares(place, mixed.shape[1])
        self.peers = range(1, place.m)

    def first(self, half, k):
        other = self.place.peer(k)
        return remote(
            self.mixed.at[half, self.lines(other)], self.got.at[half, k - 1], self.sems,
            (0, half, k - 1), {"wid": other},
        )

    def second(self, half, k):
        return remote(
            self.mine.at[half], self.proj.at[half, self.lines(self.place.wid)], self.sems,
            (1, half, k - 1), {"wid": self.place.peer(k)},
        )

    def start(self, half):
        for k in self.peers:
            self.first(half, k).start()

    def spread(self, half):
        total = self.mixed[half, self.lines(self.place.wid), :]
        for k in self.peers:
            self.first(half, k).wait_recv()
            total = total + self.got[half, k - 1]
        self.totals[half] = total
        size = total.shape[1]
        lines = slice(half * size, (half + 1) * size)
        value = jnp.zeros_like(total)
        for h in range(half + 1):
            block = self.inverse[lines, h * size : (h + 1) * size]
            value = value + nt(self.totals[h], block, HIGH)
        value = value.astype(self.mine.dtype)
        self.mine[half] = value
        for k in self.peers:
            self.second(half, k).start()
        self.proj[half, self.lines(self.place.wid), :] = value

    def finish(self):
        for half in range(HALVES):
            for k in self.peers:
                self.second(half, k).wait_recv()

    def drain(self):
        for half in range(HALVES):
            for k in self.peers:
                self.first(half, k).wait_send()
                self.second(half, k).wait_send()


class Gram:
    def __init__(self, place, part, got, share, crossed, ends, mine, gram, sems):
        self.place, self.part, self.got, self.share = place, part, got, share
        self.crossed, self.ends, self.mine, self.gram = crossed, ends, mine, gram
        self.wid_sems, self.cross_sems, self.end_sems = sems
        self.lines = shares(place, gram.shape[0])

    def first(self, k):
        other = self.place.peer(k)
        return remote(
            self.part.at[self.lines(other)], self.got.at[k - 1], self.wid_sems, (0, k - 1),
            {"wid": other},
        )

    def over_x(self):
        return remote(
            self.share, self.crossed, self.cross_sems, 0, {"tok": self.place.across}
        )

    def over_z(self, end):
        block = self.ends.at[end]
        step = -1 if end else 1
        return remote(block, block, self.end_sems, end, {"tok": self.place.along(step)})

    def spread(self, k):
        return remote(
            self.mine, self.gram.at[self.lines(self.place.wid)], self.wid_sems, (1, k - 1),
            {"wid": self.place.peer(k)},
        )

    def start(self, full):
        @pl.when(self.place.is_end)
        def _():
            rank, width = self.part.shape[0], full.shape[-1]
            unit = unit_of(self.place.end, self.place.x, 0)
            a = full[unit].reshape(rank, width)
            b = full[unit + 1].reshape(rank, width)
            self.part[...] = nt(a, a) + nt(b, b)
            for k in range(1, self.place.m):
                self.first(k).start()

    def cross(self):
        @pl.when(self.place.is_end)
        def _():
            total = self.part[self.lines(self.place.wid), :]
            for k in range(1, self.place.m):
                self.first(k).wait_recv()
                total = total + self.got[k - 1]
            self.share[...] = total
            self.over_x().start()

    def along(self):
        @pl.when(self.place.is_end)
        def _():
            self.over_x().wait_recv()
            self.ends[self.place.end] = self.share[...] + self.crossed[...]
            for end in range(ENDS):
                pl.when(self.place.end == end)(lambda: self.over_z(end).start())

    def relay(self, step):
        for end in range(ENDS):
            @pl.when(self.place.to_end(1 - end) == step)
            def _():
                self.over_z(end).wait_recv()
                if step < LAST:
                    self.over_z(end).start()

    def gather(self):
        self.relay(LAST)
        total = self.ends[0] + self.ends[1]
        self.mine[...] = total
        for k in range(1, self.place.m):
            self.spread(k).start()
        self.gram[self.lines(self.place.wid), :] = total

    def finish(self):
        for k in range(1, self.place.m):
            self.spread(k).wait_recv()

    def drain(self):
        @pl.when(self.place.is_end)
        def _():
            for k in range(1, self.place.m):
                self.first(k).wait_send()
            self.over_x().wait_send()

        for end in range(ENDS):
            pl.when(self.place.to_end(1 - end) < LAST)(
                lambda: self.over_z(end).wait_send()
            )
        for k in range(1, self.place.m):
            self.spread(k).wait_send()


def gather_sketch(place, acts, full, sums, gram, rest, right, inverse, line_sems, forward_sems, swap_sems):
    x, end = place.x, place.end
    rank, width = rest.shape[0], full.shape[-1]
    mixed, run = sums.mixed, PIECES // HALVES
    per_half = GROUPS * run
    solve_at = FILL + 29

    def spot(end_, k):
        half, rest_of = lax.div(k, per_half), lax.rem(k, per_half)
        group, piece = lax.div(rest_of, run), half * run + lax.rem(rest_of, run)
        side = jnp.where(group == GROUPS - 1, 1 - x, x)
        part = jnp.where(group == 0, 0, 1)
        return group, piece, unit_of(end_, side, part)

    def copy(unit, piece, sems, index, device):
        block = full.at[unit, piece]
        return remote(block, block, sems, index, {"tok": device})

    def line_copy(way, k):
        group, piece, unit = spot(way, k)
        return copy(unit, piece, line_sems, (way, k), place.along(-1 if way else 1))

    def forward_copy(way, piece):
        return copy(unit_of(way, x, 0), piece, forward_sems, (way, piece), place.across)

    def swap_copy(piece):
        return copy(unit_of(end, x, 1), piece, swap_sems, piece, place.across)

    def hop(way, k):
        pos = place.to_end(1 - way)
        group, piece, unit = spot(way, k)

        @pl.when(pos > 0)
        def _():
            line_copy(way, k).wait_recv()

        @pl.when(both(pos == 0, group == GROUPS - 1))
        def _():
            swap_copy(piece).wait_recv()

        @pl.when(pos < LAST)
        def _():
            line_copy(way, k).start()

    def add(half, unit):
        columns = pl.ds(pl.multiple_of(unit * width, 128), width)
        block = full[unit, half * run : (half + 1) * run]
        mixed[half] += nt(acts[:, columns], block.reshape(rank // HALVES, width))

    adds = []
    for half in range(HALVES):
        for way in WAYS:
            ready = half * per_half + FILL + way
            adds.append((ready + run, half, unit_of(way, x, 0)))
            adds.append((ready + 2 * run, half, unit_of(way, x, 1)))
            adds.append((ready + 3 * run, half, unit_of(way, 1 - x, 1)))
            adds.append((ready + (way + 2) * run + 2, half, unit_of(way, 1 - x, 0)))

    mixed[...] = jnp.zeros_like(mixed)

    def slot(s):
        @pl.when(both(place.is_end, within(s, 0, PIECES)))
        def _():
            swap_copy(s).start()

        for way in WAYS:
            k = s - SKEW * place.to_end(1 - way)
            pl.when(within(k, 0, HOPS))(functools.partial(hop, way, k))
            for half in range(HALVES):
                sent = s - FILL - half * per_half - way * run
                piece = half * run + sent
                pl.when(within(sent, 0, run))(lambda: forward_copy(way, piece).start())
                pl.when(within(sent, run, run))(
                    lambda: forward_copy(way, piece - run).wait_recv()
                )

        pl.when(s == FILL)(lambda: gram.start(full))
        pl.when(s == FILL + 4)(gram.cross)
        pl.when(s == FILL + 9)(gram.along)
        for step in range(1, LAST):
            pl.when(s == FILL + 9 + 5 * step)(lambda: gram.relay(step))
        pl.when(s == FILL + 9 + 5 * LAST)(gram.gather)

        @pl.when(s == solve_at - 1)
        def _():
            gram.finish()
            start_solve(gram.gram, rest, right)

        solve = s - solve_at
        for part in range(TURNS):
            mine = both(within(solve, 0, TURNS * PANELS), lax.rem(solve, TURNS) == part)
            pl.when(mine)(
                lambda: solve_part(lax.div(solve, TURNS), part, rest, right, inverse)
            )

        for at, half, unit in adds:
            if at < HOPS + FILL:
                pl.when(s == at)(lambda: add(half, unit))
        pl.when(s == FILL + per_half + 4)(lambda: sums.start(0))
        pl.when(s == solve_at + TURNS * PANELS // HALVES + 2)(lambda: sums.spread(0))

    def finish():
        for at, half, unit in adds:
            if at >= HOPS + FILL:
                add(half, unit)
        sums.start(1)
        sums.spread(1)
        sums.finish()

    def drain():
        for way in WAYS:
            @pl.when(place.to_end(1 - way) < LAST)
            def _():
                def one(k, carry):
                    line_copy(way, k).wait_send()
                    return carry

                lax.fori_loop(0, HOPS, one, 0)

        def one(k, carry):
            for way in WAYS:
                forward_copy(way, k).wait_send()
            pl.when(place.is_end)(lambda: swap_copy(k).wait_send())
            return carry

        lax.fori_loop(0, PIECES, one, 0)

    return slot, finish, drain


def start_solve(gram, rest, right):
    i = lax.broadcasted_iota(jnp.int32, rest.shape, 0)
    j = lax.broadcasted_iota(jnp.int32, rest.shape, 1)
    rest[...] = gram[...]
    right[...] = jnp.where(i == j, 1.0, 0.0)


def solve_part(k, part, rest, right, inverse):
    size = rest.shape[0]
    block = size // PANELS
    lane = lax.broadcasted_iota(jnp.int32, (block, size), 1)
    line = lax.broadcasted_iota(jnp.int32, (block, size), 0)
    one_line = lax.broadcasted_iota(jnp.int32, (block, 1), 0)
    first = pl.multiple_of(k * block, block)
    lines = pl.ds(first, block)
    rows, side = rest[lines, :], right[lines, :]
    count = block // TURNS
    for start in range(part * count, (part + 1) * count, STEP):
        pivots = range(start, start + STEP)
        columns = [
            jnp.sum(jnp.where(lane == first + j, rows, 0.0), axis=1, keepdims=True)
            for j in pivots
        ]
        done = []
        for c, j in enumerate(pivots):
            column, later = columns[c], columns[c + 1 :]
            one = slice(j, j + 1)
            top, beside = rows[one, :], side[one, :]
            heads = [other[one, :] for other in later]
            for ratio, its_top, its_side, its_heads in done:
                e = len(its_heads) - len(later) - 1
                column = column - ratio * its_heads[e]
                top = top - ratio[one, :] * its_top
                beside = beside - ratio[one, :] * its_side
                heads = [
                    head - ratio[one, :] * its_heads[e + 1 + i]
                    for i, head in enumerate(heads)
                ]
            ratio = jnp.where(one_line > j, column * (1.0 / column[one, :]), 0.0)
            done.append((ratio, top, beside, heads))
        for ratio, top, beside, _ in done:
            rows = rows - ratio * top
            side = side - ratio * beside
    if part < TURNS - 1:
        rest[lines, :] = rows
        right[lines, :] = side
        return
    diagonal = jnp.sum(
        jnp.where(lane == first + line, rows, 0.0), axis=1, keepdims=True
    )
    scale = 1.0 / jnp.sqrt(diagonal)
    rows = jnp.where(lane >= first + line, rows * scale, 0.0)
    side = side * scale
    inverse[lines, :] = side
    rest[...] -= tn(rows, rows, HIGH)
    right[...] -= tn(rows, side, HIGH)


class Ring:
    def __init__(self, n):
        self.n, self.rows, self.cols = n, LINE, n // LINE
        self.body = self.rows * (self.cols - 1)
        self.tok = lax.axis_index("tok")
        self.pos = self.pos_of(self.tok)

    def pos_of(self, tok):
        r, c = lax.div(tok, self.cols), lax.rem(tok, self.cols)
        odd = lax.rem(r, 2)
        inner = lax.div(c + self.cols - 1, self.cols)
        along = r * (self.cols - 1) + (1 - odd) * (c - 1) + odd * (self.cols - 1 - c)
        back = self.body + self.rows - 1 - r
        return inner * along + (1 - inner) * back

    def tok_of(self, pos):
        last = lax.div(pos, self.body)
        r, k = lax.div(pos, self.cols - 1), lax.rem(pos, self.cols - 1)
        odd = lax.rem(r, 2)
        along = r * self.cols + (1 - odd) * (k + 1) + odd * (self.cols - 1 - k)
        back = (self.rows - 1 - (pos - self.body)) * self.cols
        return (1 - last) * along + last * back

    def at(self, offset):
        return lax.rem(self.pos + offset + 2 * self.n, self.n)

    def neighbours(self):
        return self.tok_of(self.at(1)), self.tok_of(self.at(-1))


def ring_scatter(ring, prepare, term, store, send, recv, sems):
    n = ring.n
    dest = ring.neighbours()

    def copy(way, step, piece):
        return remote(
            send.at[way, step, piece], recv.at[way, step, piece], sems, (way, step, piece),
            {"tok": dest[way]},
        )

    def block(way, step):
        return ring.at(-1 - step) if way == 0 else ring.at(1 + step)

    for piece in range(RING_PIECES):
        for way in WAYS:
            prepare(way, piece)
            send[way, 0, piece] = term(way, piece, block(way, 0)).astype(BF16)
            copy(way, 0, piece).start()

    def step(s, carry):
        for piece in range(RING_PIECES):
            for way in WAYS:
                own = term(way, piece, block(way, s))
                copy(way, s - 1, piece).wait_recv()
                total = own + recv[way, s - 1, piece].astype(F32)
                send[way, s, piece] = total.astype(BF16)
                copy(way, s, piece).start()
        return carry

    lax.fori_loop(1, n - 1, step, 0)
    for piece in range(RING_PIECES):
        for way in WAYS:
            own = term(way, piece, ring.pos)
            copy(way, n - 2, piece).wait_recv()
            store(way, piece, own + recv[way, n - 2, piece].astype(F32))

    def drain(s, carry):
        for piece in range(RING_PIECES):
            for way in WAYS:
                copy(way, s, piece).wait_send()
        return carry

    lax.fori_loop(0, n - 1, drain, 0)


def coeffs(place, proj, grads, out, terms, send, recv, sems, scale):
    ring = Ring(place.n)
    rows, width = out.shape
    part = width // (2 * RING_PIECES)

    def prepare(way, piece):
        first = (way * RING_PIECES + piece) * part
        last = first + part
        count = place.n // HALVES
        for half in range(HALVES):
            value = tn(proj[half], grads[:, first:last])
            blocks = slice(half * count, (half + 1) * count)
            terms[blocks, :, first:last] = (value * scale).reshape(count, rows, part)

    def term(way, piece, pos):
        first = (way * RING_PIECES + piece) * part
        return terms[ring.tok_of(pos), :, first : first + part]

    def store(way, piece, total):
        first = (way * RING_PIECES + piece) * part
        out[:, first : first + part] = total

    ring_scatter(ring, prepare, term, store, send, recv, sems)


def kernel(n, m, scale, names, acts_in, grads_in, test_in, out, *refs):
    s = types.SimpleNamespace(**dict(zip(names, refs)))
    place = Place(n, m)
    loads = [
        pltpu.make_async_copy(src, dst, s.load_sems.at[i])
        for i, (src, dst) in enumerate(
            ((grads_in, s.grads), (test_in, s.test), (acts_in, s.acts))
        )
    ]
    for load in loads[:2]:
        load.start()
    place.barrier()
    for load in loads[:2]:
        load.wait()
    loads[2].start()
    s.probe_part[...] = jnp.dot(s.grads[...], s.test[...], preferred_element_type=F32).T
    wid_sum(
        place, s.probe_part, s.probe_got, s.probe_mine, s.probe,
        (s.probe_send, s.probe_recv), lambda total: total,
    )
    loads[2].wait()
    reduce_slot, drain_reduce = reduce_sketch(
        place, s.acts, s.probe, s.terms, s.line, s.cross, s.last, s.full,
        (s.line_send, s.line_recv), (s.cross_send, s.cross_recv), (s.last_send, s.last_recv),
    )
    gram = Gram(
        place, s.gram_part, s.gram_got, s.gram_share, s.gram_cross, s.gram_ends,
        s.gram_mine, s.gram,
        (
            (s.gram_send, s.gram_recv), (s.gram_x_send, s.gram_x_recv),
            (s.gram_z_send, s.gram_z_recv),
        ),
    )
    sums = Projections(
        place, s.mixed, s.mixed_got, s.mixed_totals, s.proj_mine, s.proj, s.inverse,
        (s.mixed_send, s.mixed_recv),
    )
    gather_slot, finish_gather, drain_gather = gather_sketch(
        place, s.acts, s.full, sums, gram, s.rest, s.right, s.inverse,
        (s.back_send, s.back_recv), (s.forward_send, s.forward_recv),
        (s.swap_send, s.swap_recv),
    )

    def slot(i, carry):
        reduce_slot(i)
        gather_slot(i - HOPS)
        return carry

    lax.fori_loop(0, SLOTS, slot, 0)
    finish_gather()
    coeffs(
        place, s.proj, s.grads, out, s.out_terms, s.ring_from, s.ring_to,
        (s.ring_send, s.ring_recv), scale,
    )
    drain_reduce()
    drain_gather()
    gram.drain()
    sums.drain()


def scratch_of(n, m, tokens, hidden, rank, model):
    units = ENDS * 2 * PARTS
    block = (rank // PIECES, hidden // units)
    vmem, dma = pltpu.VMEM, pltpu.SemaphoreType.DMA
    rows = rank // n
    part = model // (2 * RING_PIECES)

    def pair(name, shape):
        return {name + "_send": dma(shape), name + "_recv": dma(shape)}

    return {
        "acts": vmem((tokens, hidden), BF16),
        "grads": vmem((tokens, model), BF16),
        "test": vmem((model, rank), BF16),
        "load_sems": dma((3,)),
        "probe_part": vmem((rank, tokens), F32),
        "probe_got": vmem((m - 1, rank // m, tokens), F32),
        "probe_mine": vmem((rank // m, tokens), BF16),
        "probe": vmem((rank, tokens), BF16),
        **pair("probe", (2, m - 1)),
        "terms": vmem((units, PIECES, *block), BF16),
        "line": vmem((ENDS, HOPS, *block), BF16),
        "cross": vmem((ENDS, PIECES, *block), BF16),
        "last": vmem((PIECES, *block), BF16),
        "full": vmem((units, PIECES, *block), BF16),
        **pair("line", (ENDS, HOPS)),
        **pair("cross", (ENDS, PIECES)),
        **pair("last", (PIECES,)),
        "gram_part": vmem((rank, rank), F32),
        "gram_got": vmem((m - 1, rank // m, rank), F32),
        "gram_share": vmem((rank // m, rank), F32),
        "gram_cross": vmem((rank // m, rank), F32),
        "gram_ends": vmem((ENDS, rank // m, rank), F32),
        "gram_mine": vmem((rank // m, rank), F32),
        "gram": vmem((rank, rank), F32),
        **pair("gram", (2, m - 1)),
        **pair("gram_x", (1,)),
        **pair("gram_z", (ENDS,)),
        "mixed": vmem((HALVES, tokens, rank // HALVES), F32),
        "rest": vmem((rank, rank), F32),
        "right": vmem((rank, rank), F32),
        "inverse": vmem((rank, rank), F32),
        **pair("back", (ENDS, HOPS)),
        **pair("forward", (ENDS, PIECES)),
        **pair("swap", (PIECES,)),
        "mixed_got": vmem((HALVES, m - 1, tokens // m, rank // HALVES), F32),
        "mixed_totals": vmem((HALVES, tokens // m, rank // HALVES), F32),
        "proj_mine": vmem((HALVES, tokens // m, rank // HALVES), BF16),
        "proj": vmem((HALVES, tokens, rank // HALVES), BF16),
        **pair("mixed", (2, HALVES, m - 1)),
        "out_terms": vmem((n, rows, model), F32),
        "ring_from": vmem((2, n - 1, RING_PIECES, rows, part), BF16),
        "ring_to": vmem((2, n - 1, RING_PIECES, rows, part), BF16),
        **pair("ring", (2, n - 1, RING_PIECES)),
    }


def line_shards(n, m, acts, out_grads, test_matrix):
    tokens, hidden = acts.shape
    rank, model = test_matrix.shape[1], out_grads.shape[1]
    scratch = scratch_of(n, m, tokens, hidden, rank, model)
    scale = 1.0 / math.sqrt(tokens * n)
    return pl.pallas_call(
        functools.partial(kernel, n, m, scale, tuple(scratch)),
        out_shape=jax.ShapeDtypeStruct((rank // n, model), F32),
        in_specs=[pl.BlockSpec(memory_space=pl.ANY)] * 3,
        out_specs=pl.BlockSpec(memory_space=pltpu.VMEM),
        scratch_shapes=list(scratch.values()),
        compiler_params=pltpu.CompilerParams(
            collective_id=0, has_side_effects=True, vmem_limit_bytes=VMEM_LIMIT
        ),
    )(acts, out_grads, test_matrix)


def factor_inverse(gram):
    lower = jnp.linalg.cholesky(gram)
    eye_matrix = jnp.eye(gram.shape[0], dtype=F32)
    return lax.linalg.triangular_solve(lower, eye_matrix, left_side=True, lower=True)


def plain_shards(acts, out_grads, test_matrix):
    partial_probe = jnp.dot(out_grads, test_matrix, preferred_element_type=F32)
    probe = lax.psum(partial_probe, "wid").astype(BF16)
    local_sketch = lax.dot_general(
        acts, probe, (((0,), (0,)), ((), ())), preferred_element_type=F32
    )
    sketch = lax.psum(local_sketch.astype(BF16), "tok")
    gram = lax.psum(
        lax.dot_general(sketch, sketch, (((0,), (0,)), ((), ())), preferred_element_type=F32),
        "wid",
    )
    inverse = factor_inverse(gram)
    mixed = lax.psum(jnp.dot(acts, sketch, preferred_element_type=F32), "wid")
    proj = jnp.dot(mixed, inverse.T, precision=lax.Precision.HIGHEST).astype(BF16)
    scale = 1.0 / math.sqrt(acts.shape[0] * lax.axis_size("tok"))
    term = lax.dot_general(
        proj, out_grads, (((0,), (0,)), ((), ())), preferred_element_type=F32
    )
    return lax.psum_scatter(term * scale, "tok", scatter_dimension=0, tiled=True)


def solution(mesh):
    n, m = mesh.shape["tok"], mesh.shape["wid"]

    def shards(acts, out_grads, test_matrix):
        tokens, hidden = acts.shape
        model, rank = test_matrix.shape
        fits = (
            n == 2 * LINE
            and m > 1
            and tokens % (16 * m) == 0
            and rank % (16 * m) == 0
            and rank % (16 * PIECES) == 0
            and rank % (16 * n) == 0
            and rank % (PANELS * TURNS * STEP) == 0
            and rank % (HALVES * 128) == 0
            and hidden % (ENDS * 2 * PARTS * 128) == 0
            and model % (2 * RING_PIECES * 128) == 0
            and (tokens * hidden + 2 * rank * hidden) * 2 < VMEM_LIMIT // 2
        )
        if fits:
            return line_shards(n, m, acts, out_grads, test_matrix)
        return plain_shards(acts, out_grads, test_matrix)

    return jax.shard_map(
        shards,
        mesh=mesh,
        in_specs=(P("tok", "wid"), P("tok", "wid"), P("wid", None)),
        out_specs=P("tok", "wid"),
        check_vma=False,
    )
```
